256 devices in a mesh: branch: 2 (over core), pair: 128 (over y, x, z).
Axes of the slice: x: 4, y: 4, z: 8, core: 2. Of those that a mesh axis runs over, the one named last changes fastest.
Arguments:
- encoder_rows: bfloat16 [256, 196, 1024], P('pair'), may hold values from -6 to 6
- pair_list: int32 [512, 2], P('pair'), may hold values from 0 to 255, as said below
- embed_weight: bfloat16 [1024, 768], P('pair'), may hold values from -0.1875 to 0.1875
- self_qkv: bfloat16 [2, 768, 2304], P('branch'), may hold values from -0.21875 to 0.21875
- self_out: bfloat16 [2, 768, 768], P('branch'), may hold values from -0.21875 to 0.21875
- cross_q: bfloat16 [2, 768, 768], P('branch'), may hold values from -0.21875 to 0.21875
- cross_kv: bfloat16 [2, 768, 1536], P('branch'), may hold values from -0.21875 to 0.21875
- cross_out: bfloat16 [2, 768, 768], P('branch'), may hold values from -0.21875 to 0.21875
Outputs:
- view_sums: float32 [2, 256, 196, 768], P('branch', 'pair')
The draws below stay inside these ranges and needn't reach their ends.
Inputs may be any that keep to these rules, and one draw needn't show every extreme that they name: `pair_list`: pair p's first image (column 0) is one of the images p // 4 * 2 to p // 4 * 2 + 1, and every image is the first image of some pair. The second image (column 1) differs from the first and is one of the images (p // 4 - 1) * 2 to (p // 4 + 2) * 2 - 1, counted modulo 256; where p % 4 is 0 it is one of the images (p // 4 + 1) * 2 to (p // 4 + 2) * 2 - 1, and where p % 4 is 1 one of the images (p // 4 - 1) * 2 to p // 4 * 2 - 1, both modulo 256.
All inputs are finite; a program needn't handle non-finite values.
Results may differ from the reference program's by a relative error of at most 0.0034.
Values may be sent and summed in bfloat16 or wider, within the bound.
A program may use at most 64 MiB of HBM per device.

```python
import math
import jax
import jax.numpy as jnp
from jax import lax

E = 1024
D = 768
HEADS = 12
TOK = 196
IMG_DEV = 2
PAIR_DEV = 4
IMAGES = 256
PAIRS = 512


def draw_pair_list(key, part):
    devices = PAIRS // PAIR_DEV
    key_shift = jax.random.fold_in(key, 11)
    key_pick = jax.random.fold_in(key, 23)
    key_upper = jax.random.fold_in(key, 37)
    key_lower = jax.random.fold_in(key, 41)
    shifted = jax.random.randint(key_shift, (devices, 1), 0, IMG_DEV)
    slot_index = jnp.arange(PAIR_DEV, dtype=jnp.int32)[None, :]
    owner = jnp.arange(devices, dtype=jnp.int32)[:, None]
    first_image = owner * IMG_DEV + (slot_index + shifted) % IMG_DEV
    first_place = IMG_DEV + (slot_index + shifted) % IMG_DEV
    picked = jax.random.randint(key_pick, (devices, PAIR_DEV), 0, 3 * IMG_DEV - 1)
    window_place = picked + (picked >= first_place).astype(jnp.int32)
    upper_place = 2 * IMG_DEV + jax.random.randint(key_upper, (devices, PAIR_DEV), 0, IMG_DEV)
    lower_place = jax.random.randint(key_lower, (devices, PAIR_DEV), 0, IMG_DEV)
    window_place = jnp.where(slot_index == 0, upper_place, jnp.where(slot_index == 1, lower_place, window_place))
    second_image = jnp.mod(owner * IMG_DEV - IMG_DEV + window_place, IMAGES)
    both = jnp.stack([first_image, second_image], axis=-1)
    return both.reshape(PAIRS, 2).astype(jnp.int32)


def level_of(own_key, dims, split, least, top_value):
    def one(position, parts):
        heights = jax.random.uniform(jax.random.fold_in(jax.random.fold_in(own_key, 6), position), (parts,), jnp.float32, least / len(split), top_value / len(split))
        return jnp.repeat(jnp.exp(heights), dims[position] // parts).reshape((-1,) + (1,) * (len(dims) - position - 1))

    factor_of = one(*split[0])
    for cut in split[1:]:
        factor_of = factor_of * one(*cut)
    return factor_of


def noise(own_key, extent, width, limit, split=(), held_as=jnp.bfloat16):
    drawn = jax.random.normal(own_key, extent, jnp.float32) * width
    if len(split) > 0:
        drawn = level_of(own_key, extent, split, -0.22, 0.18) * drawn
    return jnp.clip(drawn, min=-limit, max=limit).astype(held_as)


def setup_inputs(seed: int = 0) -> dict:
    keys = jax.random.split(jax.random.key(seed), 9)
    encoder_rows = noise(keys[0], (IMAGES, TOK, E), 1.0, 6.0, ((0, 128),))
    pair_list = draw_pair_list(jax.random.fold_in(keys[8], 71), 0)
    embed_weight = noise(keys[2], (E, D), E ** -0.5, 0.1875, ((0, 128),))
    self_qkv = noise(keys[3], (2, D, 3 * D), D ** -0.5, 0.21875, ((0, 2),))
    self_out = noise(keys[4], (2, D, D), D ** -0.5, 0.21875, ((0, 2),))
    cross_q = noise(keys[5], (2, D, D), D ** -0.5, 0.21875, ((0, 2),))
    cross_kv = noise(keys[6], (2, D, 2 * D), D ** -0.5, 0.21875, ((0, 2),))
    cross_out = noise(keys[7], (2, D, D), D ** -0.5, 0.21875, ((0, 2),))
    return dict(encoder_rows=encoder_rows, pair_list=pair_list, embed_weight=embed_weight, self_qkv=self_qkv, self_out=self_out, cross_q=cross_q, cross_kv=cross_kv, cross_out=cross_out)


def layer_norm(values):
    values = values.astype(jnp.float32)
    average = lax.optimization_barrier(jnp.mean(values, axis=-1, keepdims=True))
    centered = values - average
    spread = lax.optimization_barrier(jnp.mean(centered * centered, axis=-1, keepdims=True))
    return (centered * lax.rsqrt(spread + 1e-06)).astype(jnp.bfloat16)

def project(values, matrix):
    leading = values.shape[:-1]
    flattened = values.reshape(-1, values.shape[-1])
    result = jnp.dot(flattened, matrix, preferred_element_type=jnp.float32)
    return result.reshape(leading + (matrix.shape[-1],))

def attend(queries, keys_in, values_in):
    pair_count, length, model_width = queries.shape
    head_dim = model_width // HEADS
    query_heads = queries.reshape(pair_count, length, HEADS, head_dim).astype(jnp.float32)
    key_heads = keys_in.reshape(pair_count, length, HEADS, head_dim).astype(jnp.float32)
    value_heads = values_in.reshape(pair_count, length, HEADS, head_dim).astype(jnp.float32)
    scores = jnp.einsum('bqhd,bkhd->bhqk', query_heads, key_heads) * (1.0 / math.sqrt(head_dim))
    raised = jnp.exp(scores)
    attn_probs = (raised / lax.optimization_barrier(jnp.sum(raised, axis=-1, keepdims=True))).astype(jnp.bfloat16)
    mixed_rows = jnp.einsum('bhqk,bkhd->bqhd', attn_probs.astype(jnp.float32), value_heads)
    return mixed_rows.reshape(pair_count, length, model_width).astype(jnp.bfloat16)

def decode_block(own_rows, partner_rows, w_qkv, w_self, w_query, w_pair, w_cross):
    model_width = own_rows.shape[-1]
    triple = project(layer_norm(own_rows), w_qkv).astype(jnp.bfloat16)
    attended = attend(triple[..., :model_width], triple[..., model_width:2 * model_width], triple[..., 2 * model_width:])
    stream = own_rows.astype(jnp.float32) + project(attended, w_self)
    query_rows = project(layer_norm(stream), w_query).astype(jnp.bfloat16)
    pair_kv = project(layer_norm(partner_rows), w_pair).astype(jnp.bfloat16)
    crossed = attend(query_rows, pair_kv[..., :model_width], pair_kv[..., model_width:])
    return stream + project(crossed, w_cross)

def reference(encoder_rows, pair_list, embed_weight, self_qkv, self_out, cross_q, cross_kv, cross_out):
    flattened = encoder_rows.reshape(IMAGES * TOK, E)
    embedded = jnp.dot(flattened, embed_weight, preferred_element_type=jnp.float32).astype(jnp.bfloat16)
    embedded = embedded.reshape(IMAGES, TOK, D)
    grouped = pair_list.reshape(PAIRS // PAIR_DEV, PAIR_DEV, 2)

    def one_group(group_ids):
        first_rows = embedded[group_ids[:, 0]]
        second_rows = embedded[group_ids[:, 1]]
        out_first = decode_block(first_rows, second_rows, self_qkv[0], self_out[0], cross_q[0], cross_kv[0], cross_out[0])
        out_second = decode_block(second_rows, first_rows, self_qkv[1], self_out[1], cross_q[1], cross_kv[1], cross_out[1])
        return (out_first, out_second)
    decoded_first, decoded_second = lax.map(one_group, grouped)
    sum_first = jax.ops.segment_sum(decoded_first.reshape(PAIRS, TOK * D), pair_list[:, 0], num_segments=IMAGES)
    sum_second = jax.ops.segment_sum(decoded_second.reshape(PAIRS, TOK * D), pair_list[:, 1], num_segments=IMAGES)
    return jnp.stack([sum_first, sum_second]).reshape(2, IMAGES, TOK, D)
```

```python
import math

import jax
import jax.numpy as jnp
from jax import lax
from jax.sharding import PartitionSpec as P

HEADS = 12


def padded(x, sides, width):
    for axis, dim in sides:
        peers, length = (lax.axis_size(axis), x.shape[dim])
        up = [(i, (i + 1) % peers) for i in range(peers)]
        down = [(j, i) for i, j in up]
        last = lax.slice_in_dim(x, length - width, length, axis=dim)
        initial = lax.slice_in_dim(x, 0, width, axis=dim)
        before = lax.ppermute(last, axis, up)
        after = lax.ppermute(initial, axis, down)
        x = jnp.concatenate([before, x, after], axis=dim)
    return x


def branch_one_padded(x, dim, width):
    peers, length = (lax.axis_size("pair"), x.shape[dim])
    base = peers
    up = [(base + i, base + (i + 1) % peers) for i in range(peers)]
    down = [(j, i) for i, j in up]
    last = lax.slice_in_dim(x, length - width, length, axis=dim)
    initial = lax.slice_in_dim(x, 0, width, axis=dim)
    before = lax.ppermute(last, ("branch", "pair"), up)
    after = lax.ppermute(initial, ("branch", "pair"), down)
    return jnp.concatenate([before, x, after], axis=dim)


def gathered_weight(weight, branch_id, devices):
    half = weight.shape[1] // 2
    mine = lax.dynamic_slice_in_dim(weight, branch_id * half, half, 1)
    spread = jnp.broadcast_to(mine[None], (devices,) + mine.shape)
    got = lax.all_to_all(spread, "pair", 0, 0, tiled=True).reshape(-1, half)
    other = lax.ppermute(got, "branch", [(0, 1), (1, 0)])
    return jnp.where(
        branch_id == 0, jnp.concatenate([got, other], 1), jnp.concatenate([other, got], 1)
    )


def swapped(value, axis, bit):
    mask = 2**bit
    pairs = [(source, source ^ mask) for source in range(lax.axis_size(axis))]
    return lax.ppermute(value, axis, pairs)


def layer_norm(values):
    values = values.astype(jnp.float32)
    average = jnp.mean(values, axis=-1, keepdims=True)
    centered = values - average
    spread = jnp.mean(centered * centered, axis=-1, keepdims=True)
    return (centered * lax.rsqrt(spread + 1e-06)).astype(jnp.bfloat16)


def project(values, matrix):
    leading = values.shape[:-1]
    flattened = values.reshape(-1, values.shape[-1])
    result = jnp.dot(flattened, matrix, preferred_element_type=jnp.float32)
    return result.reshape(leading + (matrix.shape[-1],))


def attend(queries, keys_in, values_in):
    pair_count, length, model_width = queries.shape
    head_dim = model_width // HEADS
    query_heads = queries.reshape(pair_count, length, HEADS, head_dim)
    key_heads = keys_in.reshape(pair_count, length, HEADS, head_dim)
    value_heads = values_in.reshape(pair_count, length, HEADS, head_dim)
    scores = jnp.einsum(
        "bqhd,bkhd->bhqk", query_heads, key_heads, preferred_element_type=jnp.float32
    ) * (1.0 / math.sqrt(head_dim))
    raised = jnp.exp(scores)
    attn_probs = (raised / jnp.sum(raised, axis=-1, keepdims=True)).astype(jnp.bfloat16)
    mixed_rows = jnp.einsum(
        "bhqk,bkhd->bqhd", attn_probs, value_heads, preferred_element_type=jnp.float32
    )
    return mixed_rows.reshape(pair_count, length, model_width).astype(jnp.bfloat16)


def attention_part(own_rows, partner_rows, w_qkv, w_self, w_query, w_pair, w_cross):
    model_width = own_rows.shape[-1]
    triple = project(layer_norm(own_rows), w_qkv).astype(jnp.bfloat16)
    attended = attend(
        triple[..., :model_width],
        triple[..., model_width : 2 * model_width],
        triple[..., 2 * model_width :],
    )
    stream = own_rows.astype(jnp.float32) + project(attended, w_self)
    query_rows = project(layer_norm(stream), w_query).astype(jnp.bfloat16)
    pair_kv = project(layer_norm(partner_rows), w_pair).astype(jnp.bfloat16)
    crossed = attend(query_rows, pair_kv[..., :model_width], pair_kv[..., model_width:])
    return stream + project(crossed, w_cross)


def select_rows(onehot, window):
    return jnp.dot(onehot.astype(jnp.bfloat16), window, preferred_element_type=jnp.float32).astype(
        jnp.bfloat16
    )


def embed_picked(onehot, window, full_embed, pair_count, tokens_per, enc_width, model_width):
    picked = select_rows(onehot, window).reshape(pair_count * tokens_per, enc_width)
    embedded_rows = jnp.dot(picked, full_embed, preferred_element_type=jnp.float32).astype(
        jnp.bfloat16
    )
    return embedded_rows.reshape(pair_count, tokens_per, model_width)


def body(encoder_rows, pair_list, embed_weight, self_qkv, self_out, cross_q, cross_kv, cross_out):
    img_local = encoder_rows.shape[0]
    tokens_per = encoder_rows.shape[1]
    enc_width = encoder_rows.shape[2]
    pair_count = pair_list.shape[0]
    views_local = self_qkv.shape[0]
    devices = lax.axis_size("pair")
    device_id = lax.axis_index("pair")
    branch_id = lax.axis_index("branch")
    image_total = img_local * devices
    window_start = (device_id - 1) * img_local
    slot_index = jnp.arange(3 * img_local, dtype=jnp.int32)
    other_onehots = []
    local_view = 0
    view_id = branch_id * views_local + local_view
    own_ids = jnp.where(view_id == 0, pair_list[:, 0], pair_list[:, 1])
    other_ids = jnp.where(view_id == 0, pair_list[:, 1], pair_list[:, 0])
    own_place = jnp.mod(own_ids - window_start, image_total)
    other_place = jnp.mod(other_ids - window_start, image_total)
    own_places = [own_place]
    own_onehots = own_place[:, None] == slot_index[None, :]
    other_onehots.append(other_place[:, None] == slot_index[None, :])
    full_embed = gathered_weight(embed_weight, branch_id, devices)
    model_width = full_embed.shape[1]
    raw_local = encoder_rows.reshape(img_local, tokens_per * enc_width)
    window = branch_one_padded(raw_local, 0, img_local)
    own_list = [
        embed_picked(
            own_onehots, window, full_embed, pair_count, tokens_per, enc_width, model_width
        )
    ]
    partner_list = [swapped(own_list[0], "branch", 0)]
    local_view = 0
    decoded = attention_part(
        own_list[local_view],
        partner_list[local_view],
        self_qkv[local_view],
        self_out[local_view],
        cross_q[local_view],
        cross_kv[local_view],
        cross_out[local_view],
    )
    place_onehot = (slot_index[:, None] == own_places[local_view][None, :]).astype(jnp.float32)
    contribution_list = [
        jnp.dot(
            place_onehot,
            decoded.reshape(pair_count, tokens_per * model_width),
            precision=lax.Precision.HIGHEST,
        )
    ]
    contributions = jnp.stack(contribution_list, axis=0)
    rim_rows = jnp.concatenate(
        [contributions[:, :img_local], contributions[:, 2 * img_local :]], axis=1
    )
    extended = branch_one_padded(rim_rows, 1, img_local)
    image_sums = (
        contributions[:, img_local : 2 * img_local]
        + extended[:, :img_local]
        + extended[:, 3 * img_local :]
    )
    return image_sums.reshape(views_local, img_local, tokens_per, model_width)


def solution(mesh):
    placed = (
        P("pair", None, None),
        P("pair", None),
        P("pair", None),
        P("branch", None, None),
        P("branch", None, None),
        P("branch", None, None),
        P("branch", None, None),
        P("branch", None, None),
    )
    return jax.shard_map(
        body, mesh=mesh, in_specs=placed, out_specs=P("branch", "pair", None, None), check_vma=False
    )
```

```python
import math

import jax
import jax.numpy as jnp
from jax import lax
from jax.sharding import PartitionSpec as P

HEADS = 12


def padded(x, sides, width):
    for axis, dim in sides:
        peers, length = (lax.axis_size(axis), x.shape[dim])
        up = [(i, (i + 1) % peers) for i in range(peers)]
        down = [(j, i) for i, j in up]
        last = lax.slice_in_dim(x, length - width, length, axis=dim)
        initial = lax.slice_in_dim(x, 0, width, axis=dim)
        before = lax.ppermute(last, axis, up)
        after = lax.ppermute(initial, axis, down)
        x = jnp.concatenate([before, x, after], axis=dim)
    return x


def branch_one_padded(x, dim, width):
    peers, length = (lax.axis_size("pair"), x.shape[dim])
    base = peers
    up = [(base + i, base + (i + 1) % peers) for i in range(peers)]
    down = [(j, i) for i, j in up]
    last = lax.slice_in_dim(x, length - width, length, axis=dim)
    initial = lax.slice_in_dim(x, 0, width, axis=dim)
    before = lax.ppermute(last, ("branch", "pair"), up)
    after = lax.ppermute(initial, ("branch", "pair"), down)
    return jnp.concatenate([before, x, after], axis=dim)


def gathered_weight(weight, branch_id, devices):
    half = weight.shape[1] // 2
    mine = lax.dynamic_slice_in_dim(weight, branch_id * half, half, 1)
    spread = jnp.broadcast_to(mine[None], (devices,) + mine.shape)
    got = lax.all_to_all(spread, "pair", 0, 0, tiled=True).reshape(-1, half)
    other = lax.ppermute(got, "branch", [(0, 1), (1, 0)])
    return jnp.where(
        branch_id == 0, jnp.concatenate([got, other], 1), jnp.concatenate([other, got], 1)
    )


def swapped(value, axis, bit):
    mask = 2**bit
    pairs = [(source, source ^ mask) for source in range(lax.axis_size(axis))]
    return lax.ppermute(value, axis, pairs)


def layer_norm(values):
    values = values.astype(jnp.float32)
    average = jnp.mean(values, axis=-1, keepdims=True)
    centered = values - average
    spread = jnp.mean(centered * centered, axis=-1, keepdims=True)
    return (centered * lax.rsqrt(spread + 1e-06)).astype(jnp.bfloat16)


def project(values, matrix):
    leading = values.shape[:-1]
    flattened = values.reshape(-1, values.shape[-1])
    result = jnp.dot(flattened, matrix, preferred_element_type=jnp.float32)
    return result.reshape(leading + (matrix.shape[-1],))


def attend(queries, keys_in, values_in):
    pair_count, length, model_width = queries.shape
    head_dim = model_width // HEADS
    query_heads = queries.reshape(pair_count, length, HEADS, head_dim)
    key_heads = keys_in.reshape(pair_count, length, HEADS, head_dim)
    value_heads = values_in.reshape(pair_count, length, HEADS, head_dim)
    scores = jnp.einsum(
        "bqhd,bkhd->bhqk", query_heads, key_heads, preferred_element_type=jnp.float32
    ) * (1.0 / math.sqrt(head_dim))
    raised = jnp.exp(scores)
    attn_probs = (raised / jnp.sum(raised, axis=-1, keepdims=True)).astype(jnp.bfloat16)
    mixed_rows = jnp.einsum(
        "bhqk,bkhd->bqhd", attn_probs, value_heads, preferred_element_type=jnp.float32
    )
    return mixed_rows.reshape(pair_count, length, model_width).astype(jnp.bfloat16)


def attention_part(own_rows, partner_rows, w_qkv, w_self, w_query, w_pair, w_cross):
    model_width = own_rows.shape[-1]
    triple = project(layer_norm(own_rows), w_qkv).astype(jnp.bfloat16)
    attended = attend(
        triple[..., :model_width],
        triple[..., model_width : 2 * model_width],
        triple[..., 2 * model_width :],
    )
    stream = own_rows.astype(jnp.float32) + project(attended, w_self)
    query_rows = project(layer_norm(stream), w_query).astype(jnp.bfloat16)
    pair_kv = project(layer_norm(partner_rows), w_pair).astype(jnp.bfloat16)
    crossed = attend(query_rows, pair_kv[..., :model_width], pair_kv[..., model_width:])
    return stream + project(crossed, w_cross)


def select_rows(onehot, window):
    return jnp.dot(onehot.astype(jnp.bfloat16), window, preferred_element_type=jnp.float32).astype(
        jnp.bfloat16
    )


def embed_picked(places, window, full_embed, pair_count, tokens_per, enc_width, model_width):
    rows = window.reshape(window.shape[0], tokens_per, enc_width)
    picked = jnp.take(rows, places, axis=0, mode="clip").reshape(pair_count * tokens_per, enc_width)
    embedded_rows = jnp.dot(picked, full_embed, preferred_element_type=jnp.float32).astype(
        jnp.bfloat16
    )
    return embedded_rows.reshape(pair_count, tokens_per, model_width)


def body(encoder_rows, pair_list, embed_weight, self_qkv, self_out, cross_q, cross_kv, cross_out):
    img_local = encoder_rows.shape[0]
    tokens_per = encoder_rows.shape[1]
    enc_width = encoder_rows.shape[2]
    pair_count = pair_list.shape[0]
    views_local = self_qkv.shape[0]
    devices = lax.axis_size("pair")
    device_id = lax.axis_index("pair")
    branch_id = lax.axis_index("branch")
    image_total = img_local * devices
    window_start = (device_id - 1) * img_local
    slot_index = jnp.arange(3 * img_local, dtype=jnp.int32)
    other_onehots = []
    local_view = 0
    view_id = branch_id * views_local + local_view
    own_ids = jnp.where(view_id == 0, pair_list[:, 0], pair_list[:, 1])
    other_ids = jnp.where(view_id == 0, pair_list[:, 1], pair_list[:, 0])
    own_place = jnp.mod(own_ids - window_start, image_total)
    other_place = jnp.mod(other_ids - window_start, image_total)
    own_places = [own_place]
    own_onehots = own_place[:, None] == slot_index[None, :]
    other_onehots.append(other_place[:, None] == slot_index[None, :])
    full_embed = gathered_weight(embed_weight, branch_id, devices)
    model_width = full_embed.shape[1]
    raw_local = encoder_rows.reshape(img_local, tokens_per * enc_width)
    window = branch_one_padded(raw_local, 0, img_local)
    own_list = [
        embed_picked(
            own_place, window, full_embed, pair_count, tokens_per, enc_width, model_width
        )
    ]
    partner_list = [swapped(own_list[0], "branch", 0)]
    local_view = 0
    decoded = attention_part(
        own_list[local_view],
        partner_list[local_view],
        self_qkv[local_view],
        self_out[local_view],
        cross_q[local_view],
        cross_kv[local_view],
        cross_out[local_view],
    )
    place_onehot = (slot_index[:, None] == own_places[local_view][None, :]).astype(jnp.float32)
    contribution_list = [
        jnp.dot(
            place_onehot,
            decoded.reshape(pair_count, tokens_per * model_width),
            precision=lax.Precision.HIGHEST,
        )
    ]
    contributions = jnp.stack(contribution_list, axis=0)
    rim_rows = jnp.concatenate(
        [contributions[:, :img_local], contributions[:, 2 * img_local :]], axis=1
    )
    extended = branch_one_padded(rim_rows.astype(jnp.bfloat16), 1, img_local).astype(jnp.float32)
    image_sums = (
        contributions[:, img_local : 2 * img_local]
        + extended[:, :img_local]
        + extended[:, 3 * img_local :]
    )
    return image_sums.reshape(views_local, img_local, tokens_per, model_width)


def solution(mesh):
    placed = (
        P("pair", None, None),
        P("pair", None),
        P("pair", None),
        P("branch", None, None),
        P("branch", None, None),
        P("branch", None, None),
        P("branch", None, None),
        P("branch", None, None),
    )
    return jax.shard_map(
        body, mesh=mesh, in_specs=placed, out_specs=P("branch", "pair", None, None), check_vma=False
    )
```

```python
import math

import jax
import jax.numpy as jnp
from jax.experimental import pallas as pl
from jax.experimental.pallas import tpu as pltpu
from jax import lax
from jax.sharding import PartitionSpec as P

HEADS = 12


def padded(x, sides, width):
    for axis, dim in sides:
        peers, length = (lax.axis_size(axis), x.shape[dim])
        up = [(i, (i + 1) % peers) for i in range(peers)]
        down = [(j, i) for i, j in up]
        last = lax.slice_in_dim(x, length - width, length, axis=dim)
        initial = lax.slice_in_dim(x, 0, width, axis=dim)
        before = lax.ppermute(last, axis, up)
        after = lax.ppermute(initial, axis, down)
        x = jnp.concatenate([before, x, after], axis=dim)
    return x


def branch_one_padded(x, dim, width):
    peers, length = (lax.axis_size("pair"), x.shape[dim])
    base = peers
    up = [(base + i, base + (i + 1) % peers) for i in range(peers)]
    down = [(j, i) for i, j in up]
    last = lax.slice_in_dim(x, length - width, length, axis=dim)
    initial = lax.slice_in_dim(x, 0, width, axis=dim)
    before = lax.ppermute(last, ("branch", "pair"), up)
    after = lax.ppermute(initial, ("branch", "pair"), down)
    return jnp.concatenate([before, x, after], axis=dim)


def gathered_weight(weight, branch_id, devices):
    half = weight.shape[1] // 2
    mine = lax.dynamic_slice_in_dim(weight, branch_id * half, half, 1)
    spread = jnp.broadcast_to(mine[None], (devices,) + mine.shape)
    got = lax.all_to_all(spread, "pair", 0, 0, tiled=True).reshape(-1, half)
    other = lax.ppermute(got, "branch", [(0, 1), (1, 0)])
    return jnp.where(
        branch_id == 0, jnp.concatenate([got, other], 1), jnp.concatenate([other, got], 1)
    )


def swapped(value, axis, bit):
    mask = 2**bit
    pairs = [(source, source ^ mask) for source in range(lax.axis_size(axis))]
    return lax.ppermute(value, axis, pairs)


def layer_norm(values):
    values = values.astype(jnp.float32)
    average = jnp.mean(values, axis=-1, keepdims=True)
    centered = values - average
    spread = jnp.mean(centered * centered, axis=-1, keepdims=True)
    return (centered * lax.rsqrt(spread + 1e-06)).astype(jnp.bfloat16)


def project(values, matrix):
    leading = values.shape[:-1]
    flattened = values.reshape(-1, values.shape[-1])
    result = jnp.dot(flattened, matrix, preferred_element_type=jnp.float32)
    return result.reshape(leading + (matrix.shape[-1],))


def attend(queries, keys_in, values_in):
    pair_count, length, model_width = queries.shape
    head_dim = model_width // HEADS
    query_heads = queries.reshape(pair_count, length, HEADS, head_dim)
    key_heads = keys_in.reshape(pair_count, length, HEADS, head_dim)
    value_heads = values_in.reshape(pair_count, length, HEADS, head_dim)
    scores = jnp.einsum(
        "bqhd,bkhd->bhqk", query_heads, key_heads, preferred_element_type=jnp.float32
    ) * (1.0 / math.sqrt(head_dim))
    raised = jnp.exp(scores)
    attn_probs = (raised / jnp.sum(raised, axis=-1, keepdims=True)).astype(jnp.bfloat16)
    mixed_rows = jnp.einsum(
        "bhqk,bkhd->bqhd", attn_probs, value_heads, preferred_element_type=jnp.float32
    )
    return mixed_rows.reshape(pair_count, length, model_width).astype(jnp.bfloat16)


def attention_kernel(q_ref, k_ref, v_ref, o_ref):
    q = q_ref[0]
    k = k_ref[0]
    v = v_ref[0]
    lanes = lax.broadcasted_iota(jnp.int32, q.shape, 1)
    head_dim = q.shape[1] // 2
    total = None
    for i in range(2):
        keep = (lanes >= i * head_dim) & (lanes < (i + 1) * head_dim)
        q_i = jnp.where(keep, q, jnp.zeros_like(q))
        scores = lax.dot_general(
            q_i, k, (((1,), (1,)), ((), ())), preferred_element_type=jnp.float32
        ) * (1.0 / math.sqrt(head_dim))
        raised = jnp.exp(scores)
        probs = (raised / jnp.sum(raised, axis=-1, keepdims=True)).astype(jnp.bfloat16)
        v_i = jnp.where(keep, v, jnp.zeros_like(v))
        mixed = jnp.dot(probs, v_i, preferred_element_type=jnp.float32)
        total = mixed if total is None else total + mixed
    o_ref[0] = total.astype(o_ref.dtype)


def attend_blocks(q_arr, k_arr, v_arr, q_off, k_off, v_off, width):
    pair_count, length = q_arr.shape[0], q_arr.shape[1]
    lane_block = 2 * (width // HEADS)
    steps = width // lane_block
    block = (1, length, lane_block)
    flops = pair_count * HEADS * length * length * (width // HEADS) * 4 * 2
    return pl.pallas_call(
        attention_kernel,
        out_shape=jax.ShapeDtypeStruct((pair_count, length, width), jnp.bfloat16),
        grid=(pair_count, steps),
        in_specs=[
            pl.BlockSpec(block, lambda b, h: (b, 0, q_off + h)),
            pl.BlockSpec(block, lambda b, h: (b, 0, k_off + h)),
            pl.BlockSpec(block, lambda b, h: (b, 0, v_off + h)),
        ],
        out_specs=pl.BlockSpec(block, lambda b, h: (b, 0, h)),
        cost_estimate=pl.CostEstimate(
            flops=flops,
            transcendentals=pair_count * HEADS * length * length,
            bytes_accessed=4 * pair_count * length * width * 2,
        ),
    )(q_arr, k_arr, v_arr)


def attention_part(own_rows, partner_rows, w_qkv, w_self, w_query, w_pair, w_cross):
    model_width = own_rows.shape[-1]
    triple = project(layer_norm(own_rows), w_qkv).astype(jnp.bfloat16)
    blocks = model_width // (2 * (model_width // HEADS))
    attended = attend_blocks(triple, triple, triple, 0, blocks, 2 * blocks, model_width)
    stream = own_rows.astype(jnp.float32) + project(attended, w_self)
    query_rows = project(layer_norm(stream), w_query).astype(jnp.bfloat16)
    pair_kv = project(layer_norm(partner_rows), w_pair).astype(jnp.bfloat16)
    crossed = attend_blocks(query_rows, pair_kv, pair_kv, 0, 0, blocks, model_width)
    return stream + project(crossed, w_cross)


def select_rows(onehot, window):
    return jnp.dot(onehot.astype(jnp.bfloat16), window, preferred_element_type=jnp.float32).astype(
        jnp.bfloat16
    )


def embed_picked(onehot, window, full_embed, pair_count, tokens_per, enc_width, model_width):
    picked = select_rows(onehot, window).reshape(pair_count * tokens_per, enc_width)
    embedded_rows = jnp.dot(picked, full_embed, preferred_element_type=jnp.float32).astype(
        jnp.bfloat16
    )
    return embedded_rows.reshape(pair_count, tokens_per, model_width)


def body(encoder_rows, pair_list, embed_weight, self_qkv, self_out, cross_q, cross_kv, cross_out):
    img_local = encoder_rows.shape[0]
    tokens_per = encoder_rows.shape[1]
    enc_width = encoder_rows.shape[2]
    pair_count = pair_list.shape[0]
    views_local = self_qkv.shape[0]
    devices = lax.axis_size("pair")
    device_id = lax.axis_index("pair")
    branch_id = lax.axis_index("branch")
    image_total = img_local * devices
    window_start = (device_id - 1) * img_local
    slot_index = jnp.arange(3 * img_local, dtype=jnp.int32)
    other_onehots = []
    local_view = 0
    view_id = branch_id * views_local + local_view
    own_ids = jnp.where(view_id == 0, pair_list[:, 0], pair_list[:, 1])
    other_ids = jnp.where(view_id == 0, pair_list[:, 1], pair_list[:, 0])
    own_place = jnp.mod(own_ids - window_start, image_total)
    other_place = jnp.mod(other_ids - window_start, image_total)
    own_places = [own_place]
    own_onehots = own_place[:, None] == slot_index[None, :]
    other_onehots.append(other_place[:, None] == slot_index[None, :])
    full_embed = gathered_weight(embed_weight, branch_id, devices)
    model_width = full_embed.shape[1]
    raw_local = encoder_rows.reshape(img_local, tokens_per * enc_width)
    window = branch_one_padded(raw_local, 0, img_local)
    own_list = [
        embed_picked(
            own_onehots, window, full_embed, pair_count, tokens_per, enc_width, model_width
        )
    ]
    partner_list = [swapped(own_list[0], "branch", 0)]
    local_view = 0
    decoded = attention_part(
        own_list[local_view],
        partner_list[local_view],
        self_qkv[local_view],
        self_out[local_view],
        cross_q[local_view],
        cross_kv[local_view],
        cross_out[local_view],
    )
    place_onehot = (slot_index[:, None] == own_places[local_view][None, :]).astype(jnp.float32)
    contribution_list = [
        jnp.dot(
            place_onehot,
            decoded.reshape(pair_count, tokens_per * model_width),
            precision=lax.Precision.HIGHEST,
        )
    ]
    contributions = jnp.stack(contribution_list, axis=0)
    rim_rows = jnp.concatenate(
        [contributions[:, :img_local], contributions[:, 2 * img_local :]], axis=1
    )
    extended = branch_one_padded(rim_rows.astype(jnp.bfloat16), 1, img_local).astype(jnp.float32)
    image_sums = (
        contributions[:, img_local : 2 * img_local]
        + extended[:, :img_local]
        + extended[:, 3 * img_local :]
    )
    return image_sums.reshape(views_local, img_local, tokens_per, model_width)


def solution(mesh):
    placed = (
        P("pair", None, None),
        P("pair", None),
        P("pair", None),
        P("branch", None, None),
        P("branch", None, None),
        P("branch", None, None),
        P("branch", None, None),
        P("branch", None, None),
    )
    return jax.shard_map(
        body, mesh=mesh, in_specs=placed, out_specs=P("branch", "pair", None, None), check_vma=False
    )
```

```python
import math

import jax
import jax.numpy as jnp
from jax.experimental import pallas as pl
from jax.experimental.pallas import tpu as pltpu
from jax import lax
from jax.sharding import PartitionSpec as P

HEADS = 12


def padded(x, sides, width):
    for axis, dim in sides:
        peers, length = (lax.axis_size(axis), x.shape[dim])
        up = [(i, (i + 1) % peers) for i in range(peers)]
        down = [(j, i) for i, j in up]
        last = lax.slice_in_dim(x, length - width, length, axis=dim)
        initial = lax.slice_in_dim(x, 0, width, axis=dim)
        before = lax.ppermute(last, axis, up)
        after = lax.ppermute(initial, axis, down)
        x = jnp.concatenate([before, x, after], axis=dim)
    return x


def branch_one_padded(x, dim, width):
    peers, length = (lax.axis_size("pair"), x.shape[dim])
    base = peers
    up = [(base + i, base + (i + 1) % peers) for i in range(peers)]
    down = [(j, i) for i, j in up]
    last = lax.slice_in_dim(x, length - width, length, axis=dim)
    initial = lax.slice_in_dim(x, 0, width, axis=dim)
    before = lax.ppermute(last, ("branch", "pair"), up)
    after = lax.ppermute(initial, ("branch", "pair"), down)
    return jnp.concatenate([before, x, after], axis=dim)


def gathered_weight(weight, branch_id, devices):
    half = weight.shape[1] // 2
    mine = lax.dynamic_slice_in_dim(weight, branch_id * half, half, 1)
    spread = jnp.broadcast_to(mine[None], (devices,) + mine.shape)
    got = lax.all_to_all(spread, "pair", 0, 0, tiled=True).reshape(-1, half)
    other = lax.ppermute(got, "branch", [(0, 1), (1, 0)])
    return jnp.where(
        branch_id == 0, jnp.concatenate([got, other], 1), jnp.concatenate([other, got], 1)
    )


def swapped(value, axis, bit):
    mask = 2**bit
    pairs = [(source, source ^ mask) for source in range(lax.axis_size(axis))]
    return lax.ppermute(value, axis, pairs)


def layer_norm(values):
    values = values.astype(jnp.float32)
    average = jnp.mean(values, axis=-1, keepdims=True)
    centered = values - average
    spread = jnp.mean(centered * centered, axis=-1, keepdims=True)
    return (centered * lax.rsqrt(spread + 1e-06)).astype(jnp.bfloat16)


def project(values, matrix):
    leading = values.shape[:-1]
    flattened = values.reshape(-1, values.shape[-1])
    result = jnp.dot(flattened, matrix, preferred_element_type=jnp.float32)
    return result.reshape(leading + (matrix.shape[-1],))


def attend(queries, keys_in, values_in):
    pair_count, length, model_width = queries.shape
    head_dim = model_width // HEADS
    query_heads = queries.reshape(pair_count, length, HEADS, head_dim)
    key_heads = keys_in.reshape(pair_count, length, HEADS, head_dim)
    value_heads = values_in.reshape(pair_count, length, HEADS, head_dim)
    scores = jnp.einsum(
        "bqhd,bkhd->bhqk", query_heads, key_heads, preferred_element_type=jnp.float32
    ) * (1.0 / math.sqrt(head_dim))
    raised = jnp.exp(scores)
    attn_probs = (raised / jnp.sum(raised, axis=-1, keepdims=True)).astype(jnp.bfloat16)
    mixed_rows = jnp.einsum(
        "bhqk,bkhd->bqhd", attn_probs, value_heads, preferred_element_type=jnp.float32
    )
    return mixed_rows.reshape(pair_count, length, model_width).astype(jnp.bfloat16)


def attention_kernel(q_ref, k_ref, v_ref, o_ref):
    length = q_ref.shape[1]
    lane_block = 2 * (q_ref.shape[2] // HEADS)
    head_dim = lane_block // 2
    lanes = lax.broadcasted_iota(jnp.int32, (length, lane_block), 1)

    def one_block(h, carry):
        columns = pl.ds(pl.multiple_of(h * lane_block, lane_block), lane_block)
        q = q_ref[0, :, columns]
        k = k_ref[0, :, columns]
        v = v_ref[0, :, columns]
        total = None
        for i in range(2):
            keep = (lanes >= i * head_dim) & (lanes < (i + 1) * head_dim)
            q_i = jnp.where(keep, q, jnp.zeros_like(q))
            scores = lax.dot_general(
                q_i, k, (((1,), (1,)), ((), ())), preferred_element_type=jnp.float32
            ) * (1.0 / math.sqrt(head_dim))
            raised = jnp.exp(scores)
            probs = (raised / jnp.sum(raised, axis=-1, keepdims=True)).astype(jnp.bfloat16)
            v_i = jnp.where(keep, v, jnp.zeros_like(v))
            mixed = jnp.dot(probs, v_i, preferred_element_type=jnp.float32)
            total = mixed if total is None else total + mixed
        o_ref[0, :, columns] = total.astype(o_ref.dtype)
        return carry

    lax.fori_loop(0, q_ref.shape[2] // lane_block, one_block, 0)


def attend_blocks(q_arr, k_arr, v_arr, q_off, k_off, v_off, width):
    pair_count, length = q_arr.shape[0], q_arr.shape[1]
    block = (1, length, width)
    flops = pair_count * HEADS * length * length * (width // HEADS) * 4 * 2
    return pl.pallas_call(
        attention_kernel,
        out_shape=jax.ShapeDtypeStruct((pair_count, length, width), jnp.bfloat16),
        grid=(pair_count,),
        in_specs=[
            pl.BlockSpec(block, lambda b: (b, 0, q_off)),
            pl.BlockSpec(block, lambda b: (b, 0, k_off)),
            pl.BlockSpec(block, lambda b: (b, 0, v_off)),
        ],
        out_specs=pl.BlockSpec(block, lambda b: (b, 0, 0)),
        cost_estimate=pl.CostEstimate(
            flops=flops,
            transcendentals=pair_count * HEADS * length * length,
            bytes_accessed=4 * pair_count * length * width * 2,
        ),
    )(q_arr, k_arr, v_arr)


def attention_part(own_rows, partner_rows, w_qkv, w_self, w_query, w_pair, w_cross):
    model_width = own_rows.shape[-1]
    triple = project(layer_norm(own_rows), w_qkv).astype(jnp.bfloat16)
    attended = attend_blocks(triple, triple, triple, 0, 1, 2, model_width)
    stream = own_rows.astype(jnp.float32) + project(attended, w_self)
    query_rows = project(layer_norm(stream), w_query).astype(jnp.bfloat16)
    pair_kv = project(layer_norm(partner_rows), w_pair).astype(jnp.bfloat16)
    crossed = attend_blocks(query_rows, pair_kv, pair_kv, 0, 0, 1, model_width)
    return stream + project(crossed, w_cross)


def select_rows(onehot, window):
    return jnp.dot(onehot.astype(jnp.bfloat16), window, preferred_element_type=jnp.float32).astype(
        jnp.bfloat16
    )


def embed_picked(onehot, window, full_embed, pair_count, tokens_per, enc_width, model_width):
    picked = select_rows(onehot, window).reshape(pair_count * tokens_per, enc_width)
    embedded_rows = jnp.dot(picked, full_embed, preferred_element_type=jnp.float32).astype(
        jnp.bfloat16
    )
    return embedded_rows.reshape(pair_count, tokens_per, model_width)


def body(encoder_rows, pair_list, embed_weight, self_qkv, self_out, cross_q, cross_kv, cross_out):
    img_local = encoder_rows.shape[0]
    tokens_per = encoder_rows.shape[1]
    enc_width = encoder_rows.shape[2]
    pair_count = pair_list.shape[0]
    views_local = self_qkv.shape[0]
    devices = lax.axis_size("pair")
    device_id = lax.axis_index("pair")
    branch_id = lax.axis_index("branch")
    image_total = img_local * devices
    window_start = (device_id - 1) * img_local
    slot_index = jnp.arange(3 * img_local, dtype=jnp.int32)
    other_onehots = []
    local_view = 0
    view_id = branch_id * views_local + local_view
    own_ids = jnp.where(view_id == 0, pair_list[:, 0], pair_list[:, 1])
    other_ids = jnp.where(view_id == 0, pair_list[:, 1], pair_list[:, 0])
    own_place = jnp.mod(own_ids - window_start, image_total)
    other_place = jnp.mod(other_ids - window_start, image_total)
    own_places = [own_place]
    own_onehots = own_place[:, None] == slot_index[None, :]
    other_onehots.append(other_place[:, None] == slot_index[None, :])
    full_embed = gathered_weight(embed_weight, branch_id, devices)
    model_width = full_embed.shape[1]
    raw_local = encoder_rows.reshape(img_local, tokens_per * enc_width)
    window = branch_one_padded(raw_local, 0, img_local)
    own_list = [
        embed_picked(
            own_onehots, window, full_embed, pair_count, tokens_per, enc_width, model_width
        )
    ]
    partner_list = [swapped(own_list[0], "branch", 0)]
    local_view = 0
    decoded = attention_part(
        own_list[local_view],
        partner_list[local_view],
        self_qkv[local_view],
        self_out[local_view],
        cross_q[local_view],
        cross_kv[local_view],
        cross_out[local_view],
    )
    place_onehot = (slot_index[:, None] == own_places[local_view][None, :]).astype(jnp.float32)
    contribution_list = [
        jnp.dot(
            place_onehot,
            decoded.reshape(pair_count, tokens_per * model_width),
            precision=lax.Precision.HIGHEST,
        )
    ]
    contributions = jnp.stack(contribution_list, axis=0)
    rim_rows = jnp.concatenate(
        [contributions[:, :img_local], contributions[:, 2 * img_local :]], axis=1
    )
    extended = branch_one_padded(rim_rows.astype(jnp.bfloat16), 1, img_local).astype(jnp.float32)
    image_sums = (
        contributions[:, img_local : 2 * img_local]
        + extended[:, :img_local]
        + extended[:, 3 * img_local :]
    )
    return image_sums.reshape(views_local, img_local, tokens_per, model_width)


def solution(mesh):
    placed = (
        P("pair", None, None),
        P("pair", None),
        P("pair", None),
        P("branch", None, None),
        P("branch", None, None),
        P("branch", None, None),
        P("branch", None, None),
        P("branch", None, None),
    )
    return jax.shard_map(
        body, mesh=mesh, in_specs=placed, out_specs=P("branch", "pair", None, None), check_vma=False
    )
```

```python
import math

import jax
import jax.numpy as jnp
from jax import lax
from jax.sharding import PartitionSpec as P

HEADS = 12


def padded(x, sides, width):
    for axis, dim in sides:
        peers, length = (lax.axis_size(axis), x.shape[dim])
        up = [(i, (i + 1) % peers) for i in range(peers)]
        down = [(j, i) for i, j in up]
        last = lax.slice_in_dim(x, length - width, length, axis=dim)
        initial = lax.slice_in_dim(x, 0, width, axis=dim)
        before = lax.ppermute(last, axis, up)
        after = lax.ppermute(initial, axis, down)
        x = jnp.concatenate([before, x, after], axis=dim)
    return x


def branch_one_padded(x, dim, width):
    peers, length = (lax.axis_size("pair"), x.shape[dim])
    base = peers
    up = [(base + i, base + (i + 1) % peers) for i in range(peers)]
    down = [(j, i) for i, j in up]
    last = lax.slice_in_dim(x, length - width, length, axis=dim)
    initial = lax.slice_in_dim(x, 0, width, axis=dim)
    before = lax.ppermute(last, ("branch", "pair"), up)
    after = lax.ppermute(initial, ("branch", "pair"), down)
    return jnp.concatenate([before, x, after], axis=dim)


def gathered_weight(weight, branch_id, devices):
    half = weight.shape[1] // 2
    mine = lax.dynamic_slice_in_dim(weight, branch_id * half, half, 1)
    spread = jnp.broadcast_to(mine[None], (devices,) + mine.shape)
    got = lax.all_to_all(spread, "pair", 0, 0, tiled=True).reshape(-1, half)
    other = lax.ppermute(got, "branch", [(0, 1), (1, 0)])
    return jnp.where(
        branch_id == 0, jnp.concatenate([got, other], 1), jnp.concatenate([other, got], 1)
    )


def swapped(value, axis, bit):
    mask = 2**bit
    pairs = [(source, source ^ mask) for source in range(lax.axis_size(axis))]
    return lax.ppermute(value, axis, pairs)


def layer_norm(values):
    values = values.astype(jnp.float32)
    average = jnp.mean(values, axis=-1, keepdims=True)
    centered = values - average
    spread = jnp.mean(centered * centered, axis=-1, keepdims=True)
    return (centered * lax.rsqrt(spread + 1e-06)).astype(jnp.bfloat16)


def project(values, matrix):
    leading = values.shape[:-1]
    flattened = values.reshape(-1, values.shape[-1])
    result = jnp.dot(flattened, matrix, preferred_element_type=jnp.float32)
    return result.reshape(leading + (matrix.shape[-1],))


def attend(queries, keys_in, values_in):
    pair_count, length, model_width = queries.shape
    head_dim = model_width // HEADS
    query_heads = queries.reshape(pair_count, length, HEADS, head_dim)
    key_heads = keys_in.reshape(pair_count, length, HEADS, head_dim)
    value_heads = values_in.reshape(pair_count, length, HEADS, head_dim)
    scores = jnp.einsum(
        "bqhd,bkhd->bhqk", query_heads, key_heads, preferred_element_type=jnp.float32
    ) * (1.0 / math.sqrt(head_dim))
    raised = jnp.exp(scores)
    attn_probs = (raised / jnp.sum(raised, axis=-1, keepdims=True)).astype(jnp.bfloat16)
    mixed_rows = jnp.einsum(
        "bhqk,bkhd->bqhd", attn_probs, value_heads, preferred_element_type=jnp.float32
    )
    return mixed_rows.reshape(pair_count, length, model_width).astype(jnp.bfloat16)


def heads_of(values, matrix, parts):
    width = values.shape[-1]
    shaped = matrix.reshape(width, parts, HEADS, matrix.shape[-1] // (parts * HEADS))
    return jnp.einsum(
        "btd,dshe->sbhte", values, shaped, preferred_element_type=jnp.float32
    ).astype(jnp.bfloat16)


def attend_heads(query_heads, key_heads, value_heads):
    head_dim = query_heads.shape[-1]
    scores = jnp.einsum(
        "bhqe,bhke->bhqk", query_heads, key_heads, preferred_element_type=jnp.float32
    ) * (1.0 / math.sqrt(head_dim))
    raised = jnp.exp(scores)
    attn_probs = (raised / jnp.sum(raised, axis=-1, keepdims=True)).astype(jnp.bfloat16)
    return jnp.einsum(
        "bhqk,bhke->bhqe", attn_probs, value_heads, preferred_element_type=jnp.float32
    ).astype(jnp.bfloat16)


def merged(mixed, matrix):
    shaped = matrix.reshape(HEADS, mixed.shape[-1], matrix.shape[-1])
    return jnp.einsum("bhte,hed->btd", mixed, shaped, preferred_element_type=jnp.float32)


def attention_part(own_rows, partner_rows, w_qkv, w_self, w_query, w_pair, w_cross):
    triple = heads_of(layer_norm(own_rows), w_qkv, 3)
    attended = attend_heads(triple[0], triple[1], triple[2])
    stream = own_rows.astype(jnp.float32) + merged(attended, w_self)
    query_rows = heads_of(layer_norm(stream), w_query, 1)[0]
    pair_kv = heads_of(layer_norm(partner_rows), w_pair, 2)
    crossed = attend_heads(query_rows, pair_kv[0], pair_kv[1])
    return stream + merged(crossed, w_cross)


def select_rows(onehot, window):
    return jnp.dot(onehot.astype(jnp.bfloat16), window, preferred_element_type=jnp.float32).astype(
        jnp.bfloat16
    )


def embed_picked(places, window, full_embed, pair_count, tokens_per, enc_width, model_width):
    rows = window.reshape(window.shape[0], tokens_per, enc_width)
    picked = jnp.take(rows, places, axis=0, mode="clip").reshape(pair_count * tokens_per, enc_width)
    embedded_rows = jnp.dot(picked, full_embed, preferred_element_type=jnp.float32).astype(
        jnp.bfloat16
    )
    return embedded_rows.reshape(pair_count, tokens_per, model_width)


def body(encoder_rows, pair_list, embed_weight, self_qkv, self_out, cross_q, cross_kv, cross_out):
    img_local = encoder_rows.shape[0]
    tokens_per = encoder_rows.shape[1]
    enc_width = encoder_rows.shape[2]
    pair_count = pair_list.shape[0]
    views_local = self_qkv.shape[0]
    devices = lax.axis_size("pair")
    device_id = lax.axis_index("pair")
    branch_id = lax.axis_index("branch")
    image_total = img_local * devices
    window_start = (device_id - 1) * img_local
    slot_index = jnp.arange(3 * img_local, dtype=jnp.int32)
    other_onehots = []
    local_view = 0
    view_id = branch_id * views_local + local_view
    own_ids = jnp.where(view_id == 0, pair_list[:, 0], pair_list[:, 1])
    other_ids = jnp.where(view_id == 0, pair_list[:, 1], pair_list[:, 0])
    own_place = jnp.mod(own_ids - window_start, image_total)
    other_place = jnp.mod(other_ids - window_start, image_total)
    own_places = [own_place]
    own_onehots = own_place[:, None] == slot_index[None, :]
    other_onehots.append(other_place[:, None] == slot_index[None, :])
    full_embed = gathered_weight(embed_weight, branch_id, devices)
    model_width = full_embed.shape[1]
    raw_local = encoder_rows.reshape(img_local, tokens_per * enc_width)
    window = branch_one_padded(raw_local, 0, img_local)
    own_list = [
        embed_picked(
            own_place, window, full_embed, pair_count, tokens_per, enc_width, model_width
        )
    ]
    partner_list = [swapped(own_list[0], "branch", 0)]
    local_view = 0
    decoded = attention_part(
        own_list[local_view],
        partner_list[local_view],
        self_qkv[local_view],
        self_out[local_view],
        cross_q[local_view],
        cross_kv[local_view],
        cross_out[local_view],
    )
    place_onehot = (slot_index[:, None] == own_places[local_view][None, :]).astype(jnp.float32)
    contribution_list = [
        jnp.dot(
            place_onehot,
            decoded.reshape(pair_count, tokens_per * model_width),
            precision=lax.Precision.HIGHEST,
        )
    ]
    contributions = jnp.stack(contribution_list, axis=0)
    rim_rows = jnp.concatenate(
        [contributions[:, :img_local], contributions[:, 2 * img_local :]], axis=1
    )
    extended = branch_one_padded(rim_rows.astype(jnp.bfloat16), 1, img_local).astype(jnp.float32)
    image_sums = (
        contributions[:, img_local : 2 * img_local]
        + extended[:, :img_local]
        + extended[:, 3 * img_local :]
    )
    return image_sums.reshape(views_local, img_local, tokens_per, model_width)


def solution(mesh):
    placed = (
        P("pair", None, None),
        P("pair", None),
        P("pair", None),
        P("branch", None, None),
        P("branch", None, None),
        P("branch", None, None),
        P("branch", None, None),
        P("branch", None, None),
    )
    return jax.shard_map(
        body, mesh=mesh, in_specs=placed, out_specs=P("branch", "pair", None, None), check_vma=False
    )
```

```python
import math

import jax
import jax.numpy as jnp
from jax import lax
from jax.sharding import PartitionSpec as P

HEADS = 12


def padded(x, sides, width):
    for axis, dim in sides:
        peers, length = (lax.axis_size(axis), x.shape[dim])
        up = [(i, (i + 1) % peers) for i in range(peers)]
        down = [(j, i) for i, j in up]
        last = lax.slice_in_dim(x, length - width, length, axis=dim)
        initial = lax.slice_in_dim(x, 0, width, axis=dim)
        before = lax.ppermute(last, axis, up)
        after = lax.ppermute(initial, axis, down)
        x = jnp.concatenate([before, x, after], axis=dim)
    return x


def branch_one_padded(x, dim, width):
    peers, length = (lax.axis_size("pair"), x.shape[dim])
    base = peers
    up = [(base + i, base + (i + 1) % peers) for i in range(peers)]
    down = [(j, i) for i, j in up]
    last = lax.slice_in_dim(x, length - width, length, axis=dim)
    initial = lax.slice_in_dim(x, 0, width, axis=dim)
    before = lax.ppermute(last, ("branch", "pair"), up)
    after = lax.ppermute(initial, ("branch", "pair"), down)
    return jnp.concatenate([before, x, after], axis=dim)


def gathered_weight(weight, branch_id, devices):
    half = weight.shape[1] // 2
    mine = lax.dynamic_slice_in_dim(weight, branch_id * half, half, 1)
    spread = jnp.broadcast_to(mine[None], (devices,) + mine.shape)
    got = lax.all_to_all(spread, "pair", 0, 0, tiled=True).reshape(-1, half)
    other = lax.ppermute(got, "branch", [(0, 1), (1, 0)])
    return jnp.where(
        branch_id == 0, jnp.concatenate([got, other], 1), jnp.concatenate([other, got], 1)
    )


def swapped(value, axis, bit):
    mask = 2**bit
    pairs = [(source, source ^ mask) for source in range(lax.axis_size(axis))]
    return lax.ppermute(value, axis, pairs)


def layer_norm(values):
    values = values.astype(jnp.float32)
    average = jnp.mean(values, axis=-1, keepdims=True)
    centered = values - average
    spread = jnp.mean(centered * centered, axis=-1, keepdims=True)
    return (centered * lax.rsqrt(spread + 1e-06)).astype(jnp.bfloat16)


def project(values, matrix):
    leading = values.shape[:-1]
    flattened = values.reshape(-1, values.shape[-1])
    result = jnp.dot(flattened, matrix, preferred_element_type=jnp.float32)
    return result.reshape(leading + (matrix.shape[-1],))


def attend(queries, keys_in, values_in):
    pair_count, length, model_width = queries.shape
    head_dim = model_width // HEADS
    query_heads = queries.reshape(pair_count, length, HEADS, head_dim)
    key_heads = keys_in.reshape(pair_count, length, HEADS, head_dim)
    value_heads = values_in.reshape(pair_count, length, HEADS, head_dim)
    scores = jnp.einsum(
        "bqhd,bkhd->bhqk", query_heads, key_heads, preferred_element_type=jnp.float32
    ) * (1.0 / math.sqrt(head_dim))
    raised = jnp.exp(scores)
    attn_probs = (raised / jnp.sum(raised, axis=-1, keepdims=True)).astype(jnp.bfloat16)
    mixed_rows = jnp.einsum(
        "bhqk,bkhd->bqhd", attn_probs, value_heads, preferred_element_type=jnp.float32
    )
    return mixed_rows.reshape(pair_count, length, model_width).astype(jnp.bfloat16)


def attention_part(own_rows, partner_rows, w_qkv, w_self, w_query, w_pair, w_cross):
    model_width = own_rows.shape[-1]
    triple = project(layer_norm(own_rows), w_qkv).astype(jnp.bfloat16)
    attended = attend(
        triple[..., :model_width],
        triple[..., model_width : 2 * model_width],
        triple[..., 2 * model_width :],
    )
    stream = own_rows.astype(jnp.float32) + project(attended, w_self)
    query_rows = project(layer_norm(stream), w_query).astype(jnp.bfloat16)
    pair_kv = project(layer_norm(partner_rows), w_pair).astype(jnp.bfloat16)
    crossed = attend(query_rows, pair_kv[..., :model_width], pair_kv[..., model_width:])
    return stream + project(crossed, w_cross)


def select_rows(onehot, window):
    return jnp.dot(onehot.astype(jnp.bfloat16), window, preferred_element_type=jnp.float32).astype(
        jnp.bfloat16
    )


def embed_picked(onehot, window, full_embed, pair_count, tokens_per, enc_width, model_width):
    picked = select_rows(onehot, window).reshape(pair_count * tokens_per, enc_width)
    embedded_rows = jnp.dot(picked, full_embed, preferred_element_type=jnp.float32).astype(
        jnp.bfloat16
    )
    return embedded_rows.reshape(pair_count, tokens_per, model_width)


def body(encoder_rows, pair_list, embed_weight, self_qkv, self_out, cross_q, cross_kv, cross_out):
    img_local = encoder_rows.shape[0]
    tokens_per = encoder_rows.shape[1]
    enc_width = encoder_rows.shape[2]
    pair_count = pair_list.shape[0]
    views_local = self_qkv.shape[0]
    devices = lax.axis_size("pair")
    device_id = lax.axis_index("pair")
    branch_id = lax.axis_index("branch")
    image_total = img_local * devices
    window_start = (device_id - 1) * img_local
    slot_index = jnp.arange(3 * img_local, dtype=jnp.int32)
    other_onehots = []
    local_view = 0
    view_id = branch_id * views_local + local_view
    own_ids = jnp.where(view_id == 0, pair_list[:, 0], pair_list[:, 1])
    other_ids = jnp.where(view_id == 0, pair_list[:, 1], pair_list[:, 0])
    own_place = jnp.mod(own_ids - window_start, image_total)
    other_place = jnp.mod(other_ids - window_start, image_total)
    own_places = [own_place]
    own_onehots = own_place[:, None] == slot_index[None, :]
    other_onehots.append(other_place[:, None] == slot_index[None, :])
    full_embed = gathered_weight(embed_weight, branch_id, devices)
    model_width = full_embed.shape[1]
    raw_local = encoder_rows.reshape(img_local, tokens_per * enc_width)
    window = branch_one_padded(raw_local, 0, img_local)
    own_list = [
        embed_picked(
            own_onehots, window, full_embed, pair_count, tokens_per, enc_width, model_width
        )
    ]
    partner_list = [swapped(own_list[0], "branch", 0)]
    local_view = 0
    decoded = attention_part(
        own_list[local_view],
        partner_list[local_view],
        self_qkv[local_view],
        self_out[local_view],
        cross_q[local_view],
        cross_kv[local_view],
        cross_out[local_view],
    )
    place_onehot = (slot_index[:, None] == own_places[local_view][None, :]).astype(jnp.float32)
    contribution_list = [
        jnp.dot(
            place_onehot,
            decoded.reshape(pair_count, tokens_per * model_width),
            precision=lax.Precision.HIGHEST,
        )
    ]
    contributions = jnp.stack(contribution_list, axis=0)
    rim_rows = jnp.concatenate(
        [contributions[:, :img_local], contributions[:, 2 * img_local :]], axis=1
    )
    extended = branch_one_padded(rim_rows.astype(jnp.bfloat16), 1, img_local).astype(jnp.float32)
    image_sums = (
        contributions[:, img_local : 2 * img_local]
        + extended[:, :img_local]
        + extended[:, 3 * img_local :]
    )
    return image_sums.reshape(views_local, img_local, tokens_per, model_width)


def solution(mesh):
    placed = (
        P("pair", None, None),
        P("pair", None),
        P("pair", None),
        P("branch", None, None),
        P("branch", None, None),
        P("branch", None, None),
        P("branch", None, None),
        P("branch", None, None),
    )
    return jax.shard_map(
        body, mesh=mesh, in_specs=placed, out_specs=P("branch", "pair", None, None), check_vma=False
    )
```

```python
import math

import jax
import jax.numpy as jnp
from jax import lax
from jax.sharding import PartitionSpec as P

HEADS = 12


def padded(x, sides, width):
    for axis, dim in sides:
        peers, length = (lax.axis_size(axis), x.shape[dim])
        up = [(i, (i + 1) % peers) for i in range(peers)]
        down = [(j, i) for i, j in up]
        last = lax.slice_in_dim(x, length - width, length, axis=dim)
        initial = lax.slice_in_dim(x, 0, width, axis=dim)
        before = lax.ppermute(last, axis, up)
        after = lax.ppermute(initial, axis, down)
        x = jnp.concatenate([before, x, after], axis=dim)
    return x


def branch_one_padded(x, dim, width):
    peers, length = (lax.axis_size("pair"), x.shape[dim])
    base = peers
    up = [(base + i, base + (i + 1) % peers) for i in range(peers)]
    down = [(j, i) for i, j in up]
    last = lax.slice_in_dim(x, length - width, length, axis=dim)
    initial = lax.slice_in_dim(x, 0, width, axis=dim)
    before = lax.ppermute(last, ("branch", "pair"), up)
    after = lax.ppermute(initial, ("branch", "pair"), down)
    return jnp.concatenate([before, x, after], axis=dim)


def gathered_weight(weight, branch_id, devices):
    half = weight.shape[1] // 2
    mine = lax.dynamic_slice_in_dim(weight, branch_id * half, half, 1)
    spread = jnp.broadcast_to(mine[None], (devices,) + mine.shape)
    got = lax.all_to_all(spread, "pair", 0, 0, tiled=True).reshape(-1, half)
    other = lax.ppermute(got, "branch", [(0, 1), (1, 0)])
    return jnp.where(
        branch_id == 0, jnp.concatenate([got, other], 1), jnp.concatenate([other, got], 1)
    )


def swapped(value, axis, bit):
    mask = 2**bit
    pairs = [(source, source ^ mask) for source in range(lax.axis_size(axis))]
    return lax.ppermute(value, axis, pairs)


def layer_norm(values):
    values = values.astype(jnp.float32)
    average = jnp.mean(values, axis=-1, keepdims=True)
    centered = values - average
    spread = jnp.mean(centered * centered, axis=-1, keepdims=True)
    return (centered * lax.rsqrt(spread + 1e-06)).astype(jnp.bfloat16)


def project(values, matrix):
    return jnp.einsum("btd,de->bte", values, matrix, preferred_element_type=jnp.float32)


def attend(queries, keys_in, values_in):
    pair_count, length, model_width = queries.shape
    head_dim = model_width // HEADS
    query_heads = queries.reshape(pair_count, length, HEADS, head_dim)
    key_heads = keys_in.reshape(pair_count, length, HEADS, head_dim)
    value_heads = values_in.reshape(pair_count, length, HEADS, head_dim)
    scores = jnp.einsum(
        "bqhd,bkhd->bhqk", query_heads, key_heads, preferred_element_type=jnp.float32
    ) * (1.0 / math.sqrt(head_dim))
    raised = jnp.exp(scores)
    attn_probs = (raised / jnp.sum(raised, axis=-1, keepdims=True)).astype(jnp.bfloat16)
    mixed_rows = jnp.einsum(
        "bhqk,bkhd->bqhd", attn_probs, value_heads, preferred_element_type=jnp.float32
    )
    return mixed_rows.reshape(pair_count, length, model_width).astype(jnp.bfloat16)


def attention_part(own_rows, partner_rows, w_qkv, w_self, w_query, w_pair, w_cross):
    model_width = own_rows.shape[-1]
    triple = project(layer_norm(own_rows), w_qkv).astype(jnp.bfloat16)
    attended = attend(
        triple[..., :model_width],
        triple[..., model_width : 2 * model_width],
        triple[..., 2 * model_width :],
    )
    stream = own_rows.astype(jnp.float32) + project(attended, w_self)
    query_rows = project(layer_norm(stream), w_query).astype(jnp.bfloat16)
    pair_kv = project(layer_norm(partner_rows), w_pair).astype(jnp.bfloat16)
    crossed = attend(query_rows, pair_kv[..., :model_width], pair_kv[..., model_width:])
    return stream + project(crossed, w_cross)


def select_rows(onehot, window):
    return jnp.einsum(
        "js,std->jtd", onehot.astype(jnp.bfloat16), window, preferred_element_type=jnp.float32
    ).astype(jnp.bfloat16)


def embed_picked(onehot, window, full_embed, pair_count, tokens_per, enc_width, model_width):
    picked = select_rows(onehot, window)
    return project(picked, full_embed).astype(jnp.bfloat16)


def body(encoder_rows, pair_list, embed_weight, self_qkv, self_out, cross_q, cross_kv, cross_out):
    img_local = encoder_rows.shape[0]
    tokens_per = encoder_rows.shape[1]
    enc_width = encoder_rows.shape[2]
    pair_count = pair_list.shape[0]
    views_local = self_qkv.shape[0]
    devices = lax.axis_size("pair")
    device_id = lax.axis_index("pair")
    branch_id = lax.axis_index("branch")
    image_total = img_local * devices
    window_start = (device_id - 1) * img_local
    slot_index = jnp.arange(3 * img_local, dtype=jnp.int32)
    other_onehots = []
    local_view = 0
    view_id = branch_id * views_local + local_view
    own_ids = jnp.where(view_id == 0, pair_list[:, 0], pair_list[:, 1])
    other_ids = jnp.where(view_id == 0, pair_list[:, 1], pair_list[:, 0])
    own_place = jnp.mod(own_ids - window_start, image_total)
    other_place = jnp.mod(other_ids - window_start, image_total)
    own_places = [own_place]
    own_onehots = own_place[:, None] == slot_index[None, :]
    other_onehots.append(other_place[:, None] == slot_index[None, :])
    full_embed = gathered_weight(embed_weight, branch_id, devices)
    model_width = full_embed.shape[1]
    window = branch_one_padded(encoder_rows, 0, img_local)
    own_list = [
        embed_picked(
            own_onehots, window, full_embed, pair_count, tokens_per, enc_width, model_width
        )
    ]
    partner_list = [swapped(own_list[0], "branch", 0)]
    local_view = 0
    decoded = attention_part(
        own_list[local_view],
        partner_list[local_view],
        self_qkv[local_view],
        self_out[local_view],
        cross_q[local_view],
        cross_kv[local_view],
        cross_out[local_view],
    )
    place_onehot = (slot_index[:, None] == own_places[local_view][None, :]).astype(jnp.float32)
    contribution_list = [
        jnp.einsum("sj,jtd->std", place_onehot, decoded, precision=lax.Precision.HIGHEST)
    ]
    contributions = jnp.stack(contribution_list, axis=0)
    rim_rows = jnp.concatenate(
        [contributions[:, :img_local], contributions[:, 2 * img_local :]], axis=1
    )
    extended = branch_one_padded(rim_rows.astype(jnp.bfloat16), 1, img_local).astype(jnp.float32)
    image_sums = (
        contributions[:, img_local : 2 * img_local]
        + extended[:, :img_local]
        + extended[:, 3 * img_local :]
    )
    return image_sums.reshape(views_local, img_local, tokens_per, model_width)


def solution(mesh):
    placed = (
        P("pair", None, None),
        P("pair", None),
        P("pair", None),
        P("branch", None, None),
        P("branch", None, None),
        P("branch", None, None),
        P("branch", None, None),
        P("branch", None, None),
    )
    return jax.shard_map(
        body, mesh=mesh, in_specs=placed, out_specs=P("branch", "pair", None, None), check_vma=False
    )
```

```python
import math

import jax
import jax.numpy as jnp
from jax import lax
from jax.sharding import PartitionSpec as P

HEADS = 12


def padded(x, sides, width):
    for axis, dim in sides:
        peers, length = (lax.axis_size(axis), x.shape[dim])
        up = [(i, (i + 1) % peers) for i in range(peers)]
        down = [(j, i) for i, j in up]
        last = lax.slice_in_dim(x, length - width, length, axis=dim)
        initial = lax.slice_in_dim(x, 0, width, axis=dim)
        before = lax.ppermute(last, axis, up)
        after = lax.ppermute(initial, axis, down)
        x = jnp.concatenate([before, x, after], axis=dim)
    return x


def branch_one_padded(x, dim, width):
    peers, length = (lax.axis_size("pair"), x.shape[dim])
    base = peers
    up = [(base + i, base + (i + 1) % peers) for i in range(peers)]
    down = [(j, i) for i, j in up]
    last = lax.slice_in_dim(x, length - width, length, axis=dim)
    initial = lax.slice_in_dim(x, 0, width, axis=dim)
    before = lax.ppermute(last, ("branch", "pair"), up)
    after = lax.ppermute(initial, ("branch", "pair"), down)
    return jnp.concatenate([before, x, after], axis=dim)


def gathered_weight(weight, branch_id, devices):
    half = weight.shape[1] // 2
    mine = lax.dynamic_slice_in_dim(weight, branch_id * half, half, 1)
    spread = jnp.broadcast_to(mine[None], (devices,) + mine.shape)
    got = lax.all_to_all(spread, "pair", 0, 0, tiled=True).reshape(-1, half)
    other = lax.ppermute(got, "branch", [(0, 1), (1, 0)])
    return jnp.where(
        branch_id == 0, jnp.concatenate([got, other], 1), jnp.concatenate([other, got], 1)
    )


def swapped(value, axis, bit):
    mask = 2**bit
    pairs = [(source, source ^ mask) for source in range(lax.axis_size(axis))]
    return lax.ppermute(value, axis, pairs)


def layer_norm(values):
    values = values.astype(jnp.float32)
    average = jnp.mean(values, axis=-1, keepdims=True)
    centered = values - average
    spread = jnp.mean(centered * centered, axis=-1, keepdims=True)
    return (centered * lax.rsqrt(spread + 1e-06)).astype(jnp.bfloat16)


def project(values, matrix):
    return jnp.einsum("btd,de->bte", values, matrix, preferred_element_type=jnp.float32)


def attend(queries, keys_in, values_in):
    pair_count, length, model_width = queries.shape
    head_dim = model_width // HEADS
    query_heads = queries.reshape(pair_count, length, HEADS, head_dim)
    key_heads = keys_in.reshape(pair_count, length, HEADS, head_dim)
    value_heads = values_in.reshape(pair_count, length, HEADS, head_dim)
    scores = jnp.einsum(
        "bqhd,bkhd->bhqk", query_heads, key_heads, preferred_element_type=jnp.float32
    ) * (1.0 / math.sqrt(head_dim))
    raised = jnp.exp(scores)
    attn_probs = (raised / jnp.sum(raised, axis=-1, keepdims=True)).astype(jnp.bfloat16)
    mixed_rows = jnp.einsum(
        "bhqk,bkhd->bqhd", attn_probs, value_heads, preferred_element_type=jnp.float32
    )
    return mixed_rows.reshape(pair_count, length, model_width).astype(jnp.bfloat16)


def attention_part(own_rows, partner_rows, w_qkv, w_self, w_query, w_pair, w_cross):
    model_width = own_rows.shape[-1]
    triple = project(layer_norm(own_rows), w_qkv).astype(jnp.bfloat16)
    attended = attend(
        triple[..., :model_width],
        triple[..., model_width : 2 * model_width],
        triple[..., 2 * model_width :],
    )
    stream = own_rows.astype(jnp.float32) + project(attended, w_self)
    query_rows = project(layer_norm(stream), w_query).astype(jnp.bfloat16)
    pair_kv = project(layer_norm(partner_rows), w_pair).astype(jnp.bfloat16)
    crossed = attend(query_rows, pair_kv[..., :model_width], pair_kv[..., model_width:])
    return stream + project(crossed, w_cross)


def select_rows(onehot, window):
    return jnp.einsum(
        "js,std->jtd", onehot.astype(jnp.bfloat16), window, preferred_element_type=jnp.float32
    ).astype(jnp.bfloat16)


def embed_picked(onehot, window, full_embed, pair_count, tokens_per, enc_width, model_width):
    picked = select_rows(onehot, window)
    return project(picked, full_embed).astype(jnp.bfloat16)


def body(encoder_rows, pair_list, embed_weight, self_qkv, self_out, cross_q, cross_kv, cross_out):
    img_local = encoder_rows.shape[0]
    tokens_per = encoder_rows.shape[1]
    enc_width = encoder_rows.shape[2]
    pair_count = pair_list.shape[0]
    views_local = self_qkv.shape[0]
    devices = lax.axis_size("pair")
    device_id = lax.axis_index("pair")
    branch_id = lax.axis_index("branch")
    image_total = img_local * devices
    window_start = (device_id - 1) * img_local
    slot_index = jnp.arange(3 * img_local, dtype=jnp.int32)
    other_onehots = []
    local_view = 0
    view_id = branch_id * views_local + local_view
    own_ids = jnp.where(view_id == 0, pair_list[:, 0], pair_list[:, 1])
    other_ids = jnp.where(view_id == 0, pair_list[:, 1], pair_list[:, 0])
    own_place = jnp.mod(own_ids - window_start, image_total)
    other_place = jnp.mod(other_ids - window_start, image_total)
    own_places = [own_place]
    own_onehots = own_place[:, None] == slot_index[None, :]
    other_onehots.append(other_place[:, None] == slot_index[None, :])
    full_embed = gathered_weight(embed_weight, branch_id, devices)
    model_width = full_embed.shape[1]
    window = branch_one_padded(encoder_rows, 0, img_local)
    own_list = [
        embed_picked(
            own_onehots, window, full_embed, pair_count, tokens_per, enc_width, model_width
        )
    ]
    partner_list = [swapped(own_list[0], "branch", 0)]
    local_view = 0
    decoded = attention_part(
        own_list[local_view],
        partner_list[local_view],
        self_qkv[local_view],
        self_out[local_view],
        cross_q[local_view],
        cross_kv[local_view],
        cross_out[local_view],
    )
    place = own_places[local_view]

    chosen = (slot_index[:, None] == place[None, :]).astype(jnp.float32)
    contributions = jnp.einsum("sj,jtd->std", chosen, decoded, precision=lax.Precision.HIGHEST)

    def slot_sums(first):
        return contributions[first : first + img_local]

    peers = lax.axis_size("pair")
    up = [(peers + i, peers + (i + 1) % peers) for i in range(peers)]
    down = [(j, i) for i, j in up]
    from_prev = lax.ppermute(slot_sums(2 * img_local).astype(jnp.bfloat16), ("branch", "pair"), up)
    from_next = lax.ppermute(slot_sums(0).astype(jnp.bfloat16), ("branch", "pair"), down)
    image_sums = (
        slot_sums(img_local) + from_prev.astype(jnp.float32) + from_next.astype(jnp.float32)
    )
    return image_sums.reshape(views_local, img_local, tokens_per, model_width)


def solution(mesh):
    placed = (
        P("pair", None, None),
        P("pair", None),
        P("pair", None),
        P("branch", None, None),
        P("branch", None, None),
        P("branch", None, None),
        P("branch", None, None),
        P("branch", None, None),
    )
    return jax.shard_map(
        body, mesh=mesh, in_specs=placed, out_specs=P("branch", "pair", None, None), check_vma=False
    )
```

```python
import math

import jax
import jax.numpy as jnp
from jax import lax
from jax.sharding import PartitionSpec as P

HEADS = 12


def padded(x, sides, width):
    for axis, dim in sides:
        peers, length = (lax.axis_size(axis), x.shape[dim])
        up = [(i, (i + 1) % peers) for i in range(peers)]
        down = [(j, i) for i, j in up]
        last = lax.slice_in_dim(x, length - width, length, axis=dim)
        initial = lax.slice_in_dim(x, 0, width, axis=dim)
        before = lax.ppermute(last, axis, up)
        after = lax.ppermute(initial, axis, down)
        x = jnp.concatenate([before, x, after], axis=dim)
    return x


def branch_one_padded(x, dim, width):
    peers, length = (lax.axis_size("pair"), x.shape[dim])
    base = peers
    up = [(base + i, base + (i + 1) % peers) for i in range(peers)]
    down = [(j, i) for i, j in up]
    last = lax.slice_in_dim(x, length - width, length, axis=dim)
    initial = lax.slice_in_dim(x, 0, width, axis=dim)
    before = lax.ppermute(last, ("branch", "pair"), up)
    after = lax.ppermute(initial, ("branch", "pair"), down)
    return jnp.concatenate([before, x, after], axis=dim)


def gathered_weight(weight, branch_id, devices):
    half = weight.shape[1] // 2
    mine = lax.dynamic_slice_in_dim(weight, branch_id * half, half, 1)
    spread = jnp.broadcast_to(mine[None], (devices,) + mine.shape)
    got = lax.all_to_all(spread, "pair", 0, 0, tiled=True).reshape(-1, half)
    other = lax.ppermute(got, "branch", [(0, 1), (1, 0)])
    return jnp.where(
        branch_id == 0, jnp.concatenate([got, other], 1), jnp.concatenate([other, got], 1)
    )


def swapped(value, axis, bit):
    mask = 2**bit
    pairs = [(source, source ^ mask) for source in range(lax.axis_size(axis))]
    return lax.ppermute(value, axis, pairs)


def layer_norm(values):
    values = values.astype(jnp.float32)
    average = jnp.mean(values, axis=-1, keepdims=True)
    centered = values - average
    spread = jnp.mean(centered * centered, axis=-1, keepdims=True)
    return (centered * lax.rsqrt(spread + 1e-06)).astype(jnp.bfloat16)


def project(values, matrix):
    return jnp.einsum("btd,de->bte", values, matrix, preferred_element_type=jnp.float32)


def attend(queries, keys_in, values_in):
    pair_count, length, model_width = queries.shape
    head_dim = model_width // HEADS
    query_heads = queries.reshape(pair_count, length, HEADS, head_dim)
    key_heads = keys_in.reshape(pair_count, length, HEADS, head_dim)
    value_heads = values_in.reshape(pair_count, length, HEADS, head_dim)
    scores = jnp.einsum(
        "bqhd,bkhd->bhqk", query_heads, key_heads, preferred_element_type=jnp.float32
    ) * (1.0 / math.sqrt(head_dim))
    raised = jnp.exp(scores)
    attn_probs = (raised / jnp.sum(raised, axis=-1, keepdims=True)).astype(jnp.bfloat16)
    mixed_rows = jnp.einsum(
        "bhqk,bkhd->bqhd", attn_probs, value_heads, preferred_element_type=jnp.float32
    )
    return mixed_rows.reshape(pair_count, length, model_width).astype(jnp.bfloat16)


def attention_part(own_rows, partner_rows, w_qkv, w_self, w_query, w_pair, w_cross):
    model_width = own_rows.shape[-1]
    triple = project(layer_norm(own_rows), w_qkv).astype(jnp.bfloat16)
    attended = attend(
        triple[..., :model_width],
        triple[..., model_width : 2 * model_width],
        triple[..., 2 * model_width :],
    )
    stream = own_rows.astype(jnp.float32) + project(attended, w_self)
    query_rows = project(layer_norm(stream), w_query).astype(jnp.bfloat16)
    pair_kv = project(layer_norm(partner_rows), w_pair).astype(jnp.bfloat16)
    crossed = attend(query_rows, pair_kv[..., :model_width], pair_kv[..., model_width:])
    return stream + project(crossed, w_cross)


def select_rows(onehot, window):
    return jnp.einsum(
        "js,std->jtd", onehot.astype(jnp.bfloat16), window, preferred_element_type=jnp.float32
    ).astype(jnp.bfloat16)


def embed_picked(onehot, window, full_embed, pair_count, tokens_per, enc_width, model_width):
    picked = select_rows(onehot, window)
    return project(picked, full_embed).astype(jnp.bfloat16)


def body(encoder_rows, pair_list, embed_weight, self_qkv, self_out, cross_q, cross_kv, cross_out):
    img_local = encoder_rows.shape[0]
    tokens_per = encoder_rows.shape[1]
    enc_width = encoder_rows.shape[2]
    pair_count = pair_list.shape[0]
    views_local = self_qkv.shape[0]
    devices = lax.axis_size("pair")
    device_id = lax.axis_index("pair")
    branch_id = lax.axis_index("branch")
    image_total = img_local * devices
    window_start = (device_id - 1) * img_local
    slot_index = jnp.arange(3 * img_local, dtype=jnp.int32)
    other_onehots = []
    local_view = 0
    view_id = branch_id * views_local + local_view
    own_ids = jnp.where(view_id == 0, pair_list[:, 0], pair_list[:, 1])
    other_ids = jnp.where(view_id == 0, pair_list[:, 1], pair_list[:, 0])
    own_place = jnp.mod(own_ids - window_start, image_total)
    other_place = jnp.mod(other_ids - window_start, image_total)
    own_places = [own_place]
    own_onehots = own_place[:, None] == slot_index[None, :]
    other_onehots.append(other_place[:, None] == slot_index[None, :])
    full_embed = gathered_weight(embed_weight, branch_id, devices)
    model_width = full_embed.shape[1]
    window = branch_one_padded(encoder_rows, 0, img_local)
    own_list = [
        embed_picked(
            own_onehots, window, full_embed, pair_count, tokens_per, enc_width, model_width
        )
    ]
    partner_list = [swapped(own_list[0], "branch", 0)]
    local_view = 0
    decoded = attention_part(
        own_list[local_view],
        partner_list[local_view],
        self_qkv[local_view],
        self_out[local_view],
        cross_q[local_view],
        cross_kv[local_view],
        cross_out[local_view],
    )
    place = own_places[local_view]

    chosen = (slot_index[:, None] == place[None, :]).astype(jnp.float32)
    contributions = jnp.einsum("sj,jtd->std", chosen, decoded, precision=lax.Precision.HIGHEST)

    def slot_sums(first):
        return contributions[first : first + img_local]

    peers = lax.axis_size("pair")
    up = [(peers + i, peers + (i + 1) % peers) for i in range(peers)]
    down = [(j, i) for i, j in up]
    handed = lax.ppermute(
        slot_sums(2 * img_local).astype(jnp.bfloat16),
        ("branch", "pair"),
        [(peers + i, i) for i in range(peers)],
    )
    from_prev = lax.ppermute(
        handed, ("branch", "pair"), [(i, peers + (i + 1) % peers) for i in range(peers)]
    )
    from_next = lax.ppermute(slot_sums(0).astype(jnp.bfloat16), ("branch", "pair"), down)
    image_sums = (
        slot_sums(img_local) + from_prev.astype(jnp.float32) + from_next.astype(jnp.float32)
    )
    return image_sums.reshape(views_local, img_local, tokens_per, model_width)


def solution(mesh):
    placed = (
        P("pair", None, None),
        P("pair", None),
        P("pair", None),
        P("branch", None, None),
        P("branch", None, None),
        P("branch", None, None),
        P("branch", None, None),
        P("branch", None, None),
    )
    return jax.shard_map(
        body, mesh=mesh, in_specs=placed, out_specs=P("branch", "pair", None, None), check_vma=False
    )
```

```python
import math

import jax
import jax.numpy as jnp
from jax import lax
from jax.sharding import PartitionSpec as P

HEADS = 12


def branch_one_padded(x, dim, width):
    peers, length = (lax.axis_size("pair"), x.shape[dim])
    base = peers
    up = [(base + i, base + (i + 1) % peers) for i in range(peers)]
    down = [(j, i) for i, j in up]
    last = lax.slice_in_dim(x, length - width, length, axis=dim)
    initial = lax.slice_in_dim(x, 0, width, axis=dim)
    before = lax.ppermute(last, ("branch", "pair"), up)
    after = lax.ppermute(initial, ("branch", "pair"), down)
    return jnp.concatenate([before, x, after], axis=dim)


def gathered_weight(weight, branch_id, devices):
    half = weight.shape[1] // 2
    mine = lax.dynamic_slice_in_dim(weight, branch_id * half, half, 1)
    spread = jnp.broadcast_to(mine[None], (devices,) + mine.shape)
    got = lax.all_to_all(spread, "pair", 0, 0, tiled=True).reshape(-1, half)
    other = lax.ppermute(got, "branch", [(0, 1), (1, 0)])
    return jnp.where(
        branch_id == 0, jnp.concatenate([got, other], 1), jnp.concatenate([other, got], 1)
    )


def swapped(value, axis, bit):
    mask = 2**bit
    pairs = [(source, source ^ mask) for source in range(lax.axis_size(axis))]
    return lax.ppermute(value, axis, pairs)


def layer_norm(values):
    values = values.astype(jnp.float32)
    average = jnp.mean(values, axis=-1, keepdims=True)
    centered = values - average
    spread = jnp.mean(centered * centered, axis=-1, keepdims=True)
    return (centered * lax.rsqrt(spread + 1e-06)).astype(jnp.bfloat16)


def project(values, matrix):
    return jnp.einsum("btd,de->bte", values, matrix, preferred_element_type=jnp.float32)


def attend(queries, keys_in, values_in):
    pair_count, length, model_width = queries.shape
    head_dim = model_width // HEADS
    query_heads = queries.reshape(pair_count, length, HEADS, head_dim)
    key_heads = keys_in.reshape(pair_count, length, HEADS, head_dim)
    value_heads = values_in.reshape(pair_count, length, HEADS, head_dim)
    scores = jnp.einsum(
        "bqhd,bkhd->bhqk", query_heads, key_heads, preferred_element_type=jnp.float32
    ) * (1.0 / math.sqrt(head_dim))
    raised = jnp.exp(scores)
    attn_probs = (raised / jnp.sum(raised, axis=-1, keepdims=True)).astype(jnp.bfloat16)
    mixed_rows = jnp.einsum(
        "bhqk,bkhd->bqhd", attn_probs, value_heads, preferred_element_type=jnp.float32
    )
    return mixed_rows.reshape(pair_count, length, model_width).astype(jnp.bfloat16)


def attention_part(own_rows, partner_rows, w_qkv, w_self, w_query, w_pair, w_cross):
    model_width = own_rows.shape[-1]
    triple = project(layer_norm(own_rows), w_qkv).astype(jnp.bfloat16)
    attended = attend(
        triple[..., :model_width],
        triple[..., model_width : 2 * model_width],
        triple[..., 2 * model_width :],
    )
    stream = own_rows.astype(jnp.float32) + project(attended, w_self)
    query_rows = project(layer_norm(stream), w_query).astype(jnp.bfloat16)
    pair_kv = project(layer_norm(partner_rows), w_pair).astype(jnp.bfloat16)
    crossed = attend(query_rows, pair_kv[..., :model_width], pair_kv[..., model_width:])
    return stream + project(crossed, w_cross)


def select_rows(onehot, window):
    return jnp.einsum(
        "js,std->jtd", onehot.astype(jnp.bfloat16), window, preferred_element_type=jnp.float32
    ).astype(jnp.bfloat16)


def embed_picked(onehot, window, full_embed):
    picked = select_rows(onehot, window)
    return project(picked, full_embed).astype(jnp.bfloat16)


def body(encoder_rows, pair_list, embed_weight, self_qkv, self_out, cross_q, cross_kv, cross_out):
    img_local = encoder_rows.shape[0]
    tokens_per = encoder_rows.shape[1]
    views_local = self_qkv.shape[0]
    devices = lax.axis_size("pair")
    device_id = lax.axis_index("pair")
    branch_id = lax.axis_index("branch")
    image_total = img_local * devices
    window_start = (device_id - 1) * img_local
    slot_index = jnp.arange(3 * img_local, dtype=jnp.int32)
    local_view = 0
    view_id = branch_id * views_local + local_view
    own_ids = jnp.where(view_id == 0, pair_list[:, 0], pair_list[:, 1])
    other_ids = jnp.where(view_id == 0, pair_list[:, 1], pair_list[:, 0])
    own_place = jnp.mod(own_ids - window_start, image_total)
    other_place = jnp.mod(other_ids - window_start, image_total)
    own_places = [own_place]
    own_onehots = own_place[:, None] == slot_index[None, :]
    full_embed = gathered_weight(embed_weight, branch_id, devices)
    model_width = full_embed.shape[1]
    window = branch_one_padded(encoder_rows, 0, img_local)
    own_list = [embed_picked(own_onehots, window, full_embed)]
    partner_list = [swapped(own_list[0], "branch", 0)]
    local_view = 0
    decoded = attention_part(
        own_list[local_view],
        partner_list[local_view],
        self_qkv[local_view],
        self_out[local_view],
        cross_q[local_view],
        cross_kv[local_view],
        cross_out[local_view],
    )
    place = own_places[local_view]

    chosen = (slot_index[:, None] == place[None, :]).astype(jnp.float32)
    contributions = jnp.einsum("sj,jtd->std", chosen, decoded, precision=lax.Precision.HIGHEST)

    def slot_sums(first):
        return contributions[first : first + img_local]

    peers = lax.axis_size("pair")
    up = [(peers + i, peers + (i + 1) % peers) for i in range(peers)]
    down = [(j, i) for i, j in up]
    from_prev = lax.ppermute(slot_sums(2 * img_local).astype(jnp.bfloat16), ("branch", "pair"), up)
    from_next = lax.ppermute(slot_sums(0).astype(jnp.bfloat16), ("branch", "pair"), down)
    image_sums = (
        slot_sums(img_local) + from_prev.astype(jnp.float32) + from_next.astype(jnp.float32)
    )
    return image_sums.reshape(views_local, img_local, tokens_per, model_width)


def solution(mesh):
    placed = (
        P("pair", None, None),
        P("pair", None),
        P("pair", None),
        P("branch", None, None),
        P("branch", None, None),
        P("branch", None, None),
        P("branch", None, None),
        P("branch", None, None),
    )
    return jax.shard_map(
        body, mesh=mesh, in_specs=placed, out_specs=P("branch", "pair", None, None), check_vma=False
    )
```

```python
import math

import jax
import jax.numpy as jnp
from jax import lax
from jax.sharding import PartitionSpec as P

HEADS = 12


def split_source_padded(x, width):
    peers, length = (lax.axis_size("pair"), x.shape[0])
    from_core_zero = [(i, peers + (i + 1) % peers) for i in range(peers)]
    from_core_one = [(peers + (i + 1) % peers, peers + i) for i in range(peers)]
    before = lax.ppermute(x[length - width :], ("branch", "pair"), from_core_zero)
    after = lax.ppermute(x[:width], ("branch", "pair"), from_core_one)
    return jnp.concatenate([before, x, after], axis=0)


def gathered_weight(weight, branch_id, devices):
    half = weight.shape[1] // 2
    mine = lax.dynamic_slice_in_dim(weight, branch_id * half, half, 1)
    spread = jnp.broadcast_to(mine[None], (devices,) + mine.shape)
    got = lax.all_to_all(spread, "pair", 0, 0, tiled=True).reshape(-1, half)
    other = lax.ppermute(got, "branch", [(0, 1), (1, 0)])
    return jnp.where(
        branch_id == 0, jnp.concatenate([got, other], 1), jnp.concatenate([other, got], 1)
    )


def swapped(value, axis, bit):
    mask = 2**bit
    pairs = [(source, source ^ mask) for source in range(lax.axis_size(axis))]
    return lax.ppermute(value, axis, pairs)


def layer_norm(values):
    values = values.astype(jnp.float32)
    average = jnp.mean(values, axis=-1, keepdims=True)
    centered = values - average
    spread = jnp.mean(centered * centered, axis=-1, keepdims=True)
    return (centered * lax.rsqrt(spread + 1e-06)).astype(jnp.bfloat16)


def project(values, matrix):
    return jnp.einsum("btd,de->bte", values, matrix, preferred_element_type=jnp.float32)


def attend(queries, keys_in, values_in):
    pair_count, length, model_width = queries.shape
    head_dim = model_width // HEADS
    query_heads = queries.reshape(pair_count, length, HEADS, head_dim)
    key_heads = keys_in.reshape(pair_count, length, HEADS, head_dim)
    value_heads = values_in.reshape(pair_count, length, HEADS, head_dim)
    scores = jnp.einsum(
        "bqhd,bkhd->bhqk", query_heads, key_heads, preferred_element_type=jnp.float32
    ) * (1.0 / math.sqrt(head_dim))
    raised = jnp.exp(scores)
    attn_probs = (raised / jnp.sum(raised, axis=-1, keepdims=True)).astype(jnp.bfloat16)
    mixed_rows = jnp.einsum(
        "bhqk,bkhd->bqhd", attn_probs, value_heads, preferred_element_type=jnp.float32
    )
    return mixed_rows.reshape(pair_count, length, model_width).astype(jnp.bfloat16)


def attention_part(own_rows, partner_rows, w_qkv, w_self, w_query, w_pair, w_cross):
    model_width = own_rows.shape[-1]
    triple = project(layer_norm(own_rows), w_qkv).astype(jnp.bfloat16)
    attended = attend(
        triple[..., :model_width],
        triple[..., model_width : 2 * model_width],
        triple[..., 2 * model_width :],
    )
    stream = own_rows.astype(jnp.float32) + project(attended, w_self)
    query_rows = project(layer_norm(stream), w_query).astype(jnp.bfloat16)
    pair_kv = project(layer_norm(partner_rows), w_pair).astype(jnp.bfloat16)
    crossed = attend(query_rows, pair_kv[..., :model_width], pair_kv[..., model_width:])
    return stream + project(crossed, w_cross)


def select_rows(onehot, window):
    return jnp.einsum(
        "js,std->jtd", onehot.astype(jnp.bfloat16), window, preferred_element_type=jnp.float32
    ).astype(jnp.bfloat16)


def embed_picked(onehot, window, full_embed):
    picked = select_rows(onehot, window)
    return project(picked, full_embed).astype(jnp.bfloat16)


def body(encoder_rows, pair_list, embed_weight, self_qkv, self_out, cross_q, cross_kv, cross_out):
    img_local = encoder_rows.shape[0]
    tokens_per = encoder_rows.shape[1]
    views_local = self_qkv.shape[0]
    devices = lax.axis_size("pair")
    device_id = lax.axis_index("pair")
    branch_id = lax.axis_index("branch")
    image_total = img_local * devices
    window_start = (device_id - 1) * img_local
    slot_index = jnp.arange(3 * img_local, dtype=jnp.int32)
    local_view = 0
    view_id = branch_id * views_local + local_view
    own_ids = jnp.where(view_id == 0, pair_list[:, 0], pair_list[:, 1])
    other_ids = jnp.where(view_id == 0, pair_list[:, 1], pair_list[:, 0])
    own_place = jnp.mod(own_ids - window_start, image_total)
    other_place = jnp.mod(other_ids - window_start, image_total)
    own_places = [own_place]
    own_onehots = own_place[:, None] == slot_index[None, :]
    full_embed = gathered_weight(embed_weight, branch_id, devices)
    model_width = full_embed.shape[1]
    window = split_source_padded(encoder_rows, img_local)
    own_list = [embed_picked(own_onehots, window, full_embed)]
    partner_list = [swapped(own_list[0], "branch", 0)]
    local_view = 0
    decoded = attention_part(
        own_list[local_view],
        partner_list[local_view],
        self_qkv[local_view],
        self_out[local_view],
        cross_q[local_view],
        cross_kv[local_view],
        cross_out[local_view],
    )
    place = own_places[local_view]

    chosen = (slot_index[:, None] == place[None, :]).astype(jnp.float32)
    contributions = jnp.einsum("sj,jtd->std", chosen, decoded, precision=lax.Precision.HIGHEST)

    def slot_sums(first):
        return contributions[first : first + img_local]

    peers = lax.axis_size("pair")
    up = [(peers + i, peers + (i + 1) % peers) for i in range(peers)]
    down = [(j, i) for i, j in up]
    from_prev = lax.ppermute(slot_sums(2 * img_local).astype(jnp.bfloat16), ("branch", "pair"), up)
    from_next = lax.ppermute(slot_sums(0).astype(jnp.bfloat16), ("branch", "pair"), down)
    image_sums = (
        slot_sums(img_local) + from_prev.astype(jnp.float32) + from_next.astype(jnp.float32)
    )
    return image_sums.reshape(views_local, img_local, tokens_per, model_width)


def solution(mesh):
    placed = (
        P("pair", None, None),
        P("pair", None),
        P("pair", None),
        P("branch", None, None),
        P("branch", None, None),
        P("branch", None, None),
        P("branch", None, None),
        P("branch", None, None),
    )
    return jax.shard_map(
        body, mesh=mesh, in_specs=placed, out_specs=P("branch", "pair", None, None), check_vma=False
    )
```

```python
import math

import jax
import jax.numpy as jnp
from jax import lax
from jax.sharding import PartitionSpec as P

HEADS = 12


def split_source_padded(x, width):
    peers, length = (lax.axis_size("pair"), x.shape[0])
    from_core_zero = [(i, peers + (i + 1) % peers) for i in range(peers)]
    from_core_one = [(peers + (i + 1) % peers, peers + i) for i in range(peers)]
    before = lax.ppermute(x[length - width :], ("branch", "pair"), from_core_zero)
    after = lax.ppermute(x[:width], ("branch", "pair"), from_core_one)
    return jnp.concatenate([before, x, after], axis=0)


def gathered_weight(weight, branch_id, devices):
    half = weight.shape[1] // 2
    mine = lax.dynamic_slice_in_dim(weight, branch_id * half, half, 1)
    spread = jnp.broadcast_to(mine[None], (devices,) + mine.shape)
    got = lax.all_to_all(spread, "pair", 0, 0, tiled=True).reshape(-1, half)
    other = lax.ppermute(got, "branch", [(0, 1), (1, 0)])
    return jnp.where(
        branch_id == 0, jnp.concatenate([got, other], 1), jnp.concatenate([other, got], 1)
    )


def swapped(value, axis, bit):
    mask = 2**bit
    pairs = [(source, source ^ mask) for source in range(lax.axis_size(axis))]
    return lax.ppermute(value, axis, pairs)


def layer_norm(values):
    values = values.astype(jnp.float32)
    average = jnp.mean(values, axis=-1, keepdims=True)
    centered = values - average
    spread = jnp.mean(centered * centered, axis=-1, keepdims=True)
    return (centered * lax.rsqrt(spread + 1e-06)).astype(jnp.bfloat16)


def project(values, matrix):
    return jnp.einsum("btd,de->bte", values, matrix, preferred_element_type=jnp.float32)


def attend(queries, keys_in, values_in):
    pair_count, length, model_width = queries.shape
    head_dim = model_width // HEADS
    query_heads = queries.reshape(pair_count, length, HEADS, head_dim)
    key_heads = keys_in.reshape(pair_count, length, HEADS, head_dim)
    value_heads = values_in.reshape(pair_count, length, HEADS, head_dim)
    scores = jnp.einsum(
        "bqhd,bkhd->bhqk", query_heads, key_heads, preferred_element_type=jnp.float32
    ) * (1.0 / math.sqrt(head_dim))
    raised = jnp.exp(scores)
    attn_probs = (raised / jnp.sum(raised, axis=-1, keepdims=True)).astype(jnp.bfloat16)
    mixed_rows = jnp.einsum(
        "bhqk,bkhd->bqhd", attn_probs, value_heads, preferred_element_type=jnp.float32
    )
    return mixed_rows.reshape(pair_count, length, model_width).astype(jnp.bfloat16)


def attention_part(own_rows, partner_rows, w_qkv, w_self, w_query, w_pair, w_cross):
    model_width = own_rows.shape[-1]
    triple = project(layer_norm(own_rows), w_qkv).astype(jnp.bfloat16)
    attended = attend(
        triple[..., :model_width],
        triple[..., model_width : 2 * model_width],
        triple[..., 2 * model_width :],
    )
    stream = own_rows.astype(jnp.float32) + project(attended, w_self)
    query_rows = project(layer_norm(stream), w_query).astype(jnp.bfloat16)
    pair_kv = project(layer_norm(partner_rows), w_pair).astype(jnp.bfloat16)
    crossed = attend(query_rows, pair_kv[..., :model_width], pair_kv[..., model_width:])
    return stream + project(crossed, w_cross)


def select_rows(onehot, window):
    return jnp.einsum(
        "js,std->jtd", onehot.astype(jnp.bfloat16), window, preferred_element_type=jnp.float32
    ).astype(jnp.bfloat16)


def embed_picked(onehot, window, full_embed):
    picked = select_rows(onehot, window)
    return project(picked, full_embed).astype(jnp.bfloat16)


def body(encoder_rows, pair_list, embed_weight, self_qkv, self_out, cross_q, cross_kv, cross_out):
    img_local = encoder_rows.shape[0]
    tokens_per = encoder_rows.shape[1]
    views_local = self_qkv.shape[0]
    devices = lax.axis_size("pair")
    device_id = lax.axis_index("pair")
    branch_id = lax.axis_index("branch")
    image_total = img_local * devices
    window_start = (device_id - 1) * img_local
    slot_index = jnp.arange(3 * img_local, dtype=jnp.int32)
    local_view = 0
    view_id = branch_id * views_local + local_view
    own_ids = jnp.where(view_id == 0, pair_list[:, 0], pair_list[:, 1])
    other_ids = jnp.where(view_id == 0, pair_list[:, 1], pair_list[:, 0])
    own_place = jnp.mod(own_ids - window_start, image_total)
    other_place = jnp.mod(other_ids - window_start, image_total)
    own_places = [own_place]
    own_onehots = own_place[:, None] == slot_index[None, :]
    full_embed = gathered_weight(embed_weight, branch_id, devices)
    model_width = full_embed.shape[1]
    window = split_source_padded(encoder_rows, img_local)
    own_list = [embed_picked(own_onehots, window, full_embed)]
    partner_list = [swapped(own_list[0], "branch", 0)]
    local_view = 0
    decoded = attention_part(
        own_list[local_view],
        partner_list[local_view],
        self_qkv[local_view],
        self_out[local_view],
        cross_q[local_view],
        cross_kv[local_view],
        cross_out[local_view],
    )
    place = own_places[local_view]

    chosen = (slot_index[:, None] == place[None, :]).astype(jnp.float32)
    contributions = sum(
        jnp.where(chosen[:, j, None, None] > 0, decoded[j][None], 0.0)
        for j in range(decoded.shape[0])
    )

    def slot_sums(first):
        return contributions[first : first + img_local]

    peers = lax.axis_size("pair")
    up = [(peers + i, peers + (i + 1) % peers) for i in range(peers)]
    down = [(j, i) for i, j in up]
    from_prev = lax.ppermute(slot_sums(2 * img_local).astype(jnp.bfloat16), ("branch", "pair"), up)
    from_next = lax.ppermute(slot_sums(0).astype(jnp.bfloat16), ("branch", "pair"), down)
    image_sums = (
        slot_sums(img_local) + from_prev.astype(jnp.float32) + from_next.astype(jnp.float32)
    )
    return image_sums.reshape(views_local, img_local, tokens_per, model_width)


def solution(mesh):
    placed = (
        P("pair", None, None),
        P("pair", None),
        P("pair", None),
        P("branch", None, None),
        P("branch", None, None),
        P("branch", None, None),
        P("branch", None, None),
        P("branch", None, None),
    )
    return jax.shard_map(
        body, mesh=mesh, in_specs=placed, out_specs=P("branch", "pair", None, None), check_vma=False
    )
```

```python
import math

import jax
import jax.numpy as jnp
from jax import lax
from jax.sharding import PartitionSpec as P

HEADS = 12


def split_source_padded(x, width):
    peers, length = (lax.axis_size("pair"), x.shape[0])
    from_core_zero = [(i, peers + (i + 1) % peers) for i in range(peers)]
    from_core_one = [(peers + (i + 1) % peers, peers + i) for i in range(peers)]
    before = lax.ppermute(x[length - width :], ("branch", "pair"), from_core_zero)
    after = lax.ppermute(x[:width], ("branch", "pair"), from_core_one)
    return jnp.concatenate([before, x, after], axis=0)


def gathered_weight(weight, branch_id, devices):
    half = weight.shape[1] // 2
    mine = lax.dynamic_slice_in_dim(weight, branch_id * half, half, 1)
    spread = jnp.broadcast_to(mine[None], (devices,) + mine.shape)
    got = lax.all_to_all(spread, "pair", 0, 0, tiled=True).reshape(-1, half)
    other = lax.ppermute(got, "branch", [(0, 1), (1, 0)])
    return got, other


def swapped(value, axis, bit):
    mask = 2**bit
    pairs = [(source, source ^ mask) for source in range(lax.axis_size(axis))]
    return lax.ppermute(value, axis, pairs)


def layer_norm(values):
    values = values.astype(jnp.float32)
    average = jnp.mean(values, axis=-1, keepdims=True)
    centered = values - average
    spread = jnp.mean(centered * centered, axis=-1, keepdims=True)
    return (centered * lax.rsqrt(spread + 1e-06)).astype(jnp.bfloat16)


def project(values, matrix):
    return jnp.einsum("btd,de->bte", values, matrix, preferred_element_type=jnp.float32)


def attend(queries, keys_in, values_in):
    pair_count, length, model_width = queries.shape
    head_dim = model_width // HEADS
    query_heads = queries.reshape(pair_count, length, HEADS, head_dim)
    key_heads = keys_in.reshape(pair_count, length, HEADS, head_dim)
    value_heads = values_in.reshape(pair_count, length, HEADS, head_dim)
    scores = jnp.einsum(
        "bqhd,bkhd->bhqk", query_heads, key_heads, preferred_element_type=jnp.float32
    ) * (1.0 / math.sqrt(head_dim))
    raised = jnp.exp(scores)
    attn_probs = (raised / jnp.sum(raised, axis=-1, keepdims=True)).astype(jnp.bfloat16)
    mixed_rows = jnp.einsum(
        "bhqk,bkhd->bqhd", attn_probs, value_heads, preferred_element_type=jnp.float32
    )
    return mixed_rows.reshape(pair_count, length, model_width).astype(jnp.bfloat16)


def attention_part(own_rows, partner_rows, w_qkv, w_self, w_query, w_pair, w_cross):
    model_width = own_rows.shape[-1]
    triple = project(layer_norm(own_rows), w_qkv).astype(jnp.bfloat16)
    attended = attend(
        triple[..., :model_width],
        triple[..., model_width : 2 * model_width],
        triple[..., 2 * model_width :],
    )
    stream = own_rows.astype(jnp.float32) + project(attended, w_self)
    query_rows = project(layer_norm(stream), w_query).astype(jnp.bfloat16)
    pair_kv = project(layer_norm(partner_rows), w_pair).astype(jnp.bfloat16)
    crossed = attend(query_rows, pair_kv[..., :model_width], pair_kv[..., model_width:])
    return stream + project(crossed, w_cross)


def select_rows(onehot, window):
    return jnp.einsum(
        "js,std->jtd", onehot.astype(jnp.bfloat16), window, preferred_element_type=jnp.float32
    ).astype(jnp.bfloat16)


def embed_picked(onehot, window, full_embed):
    picked = select_rows(onehot, window)
    got, other, branch_id = full_embed
    mine = project(picked, got).astype(jnp.bfloat16)
    theirs = project(picked, other).astype(jnp.bfloat16)
    return jnp.where(
        branch_id == 0, jnp.concatenate([mine, theirs], -1), jnp.concatenate([theirs, mine], -1)
    )


def body(encoder_rows, pair_list, embed_weight, self_qkv, self_out, cross_q, cross_kv, cross_out):
    img_local = encoder_rows.shape[0]
    tokens_per = encoder_rows.shape[1]
    views_local = self_qkv.shape[0]
    devices = lax.axis_size("pair")
    device_id = lax.axis_index("pair")
    branch_id = lax.axis_index("branch")
    image_total = img_local * devices
    window_start = (device_id - 1) * img_local
    slot_index = jnp.arange(3 * img_local, dtype=jnp.int32)
    local_view = 0
    view_id = branch_id * views_local + local_view
    own_ids = jnp.where(view_id == 0, pair_list[:, 0], pair_list[:, 1])
    other_ids = jnp.where(view_id == 0, pair_list[:, 1], pair_list[:, 0])
    own_place = jnp.mod(own_ids - window_start, image_total)
    other_place = jnp.mod(other_ids - window_start, image_total)
    own_places = [own_place]
    own_onehots = own_place[:, None] == slot_index[None, :]
    full_embed = gathered_weight(embed_weight, branch_id, devices) + (branch_id,)
    model_width = 2 * full_embed[0].shape[1]
    window = split_source_padded(encoder_rows, img_local)
    own_list = [embed_picked(own_onehots, window, full_embed)]
    partner_list = [swapped(own_list[0], "branch", 0)]
    local_view = 0
    decoded = attention_part(
        own_list[local_view],
        partner_list[local_view],
        self_qkv[local_view],
        self_out[local_view],
        cross_q[local_view],
        cross_kv[local_view],
        cross_out[local_view],
    )
    place = own_places[local_view]

    chosen = (slot_index[:, None] == place[None, :]).astype(jnp.float32)
    contributions = sum(
        jnp.where(chosen[:, j, None, None] > 0, decoded[j][None], 0.0)
        for j in range(decoded.shape[0])
    )

    def slot_sums(first):
        return contributions[first : first + img_local]

    peers = lax.axis_size("pair")
    up = [(peers + i, peers + (i + 1) % peers) for i in range(peers)]
    down = [(j, i) for i, j in up]
    from_prev = lax.ppermute(slot_sums(2 * img_local).astype(jnp.bfloat16), ("branch", "pair"), up)
    from_next = lax.ppermute(slot_sums(0).astype(jnp.bfloat16), ("branch", "pair"), down)
    image_sums = (
        slot_sums(img_local) + from_prev.astype(jnp.float32) + from_next.astype(jnp.float32)
    )
    return image_sums.reshape(views_local, img_local, tokens_per, model_width)


def solution(mesh):
    placed = (
        P("pair", None, None),
        P("pair", None),
        P("pair", None),
        P("branch", None, None),
        P("branch", None, None),
        P("branch", None, None),
        P("branch", None, None),
        P("branch", None, None),
    )
    return jax.shard_map(
        body, mesh=mesh, in_specs=placed, out_specs=P("branch", "pair", None, None), check_vma=False
    )
```
